32 devices in a mesh: dom: 8 (over z, y), rhs: 4 (over x, core).
Axes of the slice: x: 2, y: 2, z: 4, core: 2. Of those that a mesh axis runs over, the one named last changes fastest.
Arguments:
- tile_values: float32 [2048, 128, 128], P(('dom', 'rhs')), may hold values from -1 to 3, as said below
- tile_rows: int32 [2048], P(('dom', 'rhs')), may hold values from -1 to 31, as said below
- tile_cols: int32 [2048], P(('dom', 'rhs')), may hold values from 0 to 39, as said below
- send_lists: int32 [8, 2, 4], P('dom'), may hold values from 0 to 31, as said below
- replace_flags: int32 [4], replicated, may hold values from 0 to 1, as said below
- right_side: float32 [4, 256, 128], P(None, ('dom', 'rhs')), may hold values from -25 to 25
- start_iterate: float32 [4, 256, 128], P(None, ('dom', 'rhs')), may hold values from -25 to 25
- start_residual: float32 [4, 256, 128], P(None, ('dom', 'rhs')), may hold values from -25 to 25
- start_direction: float32 [4, 256, 128], P(None, ('dom', 'rhs')), may hold values from -25 to 25
Outputs:
- new_iterate: float32 [4, 256, 128], P(None, ('dom', 'rhs'))
- new_residual: float32 [4, 256, 128], P(None, ('dom', 'rhs'))
- new_direction: float32 [4, 256, 128], P(None, ('dom', 'rhs'))
The draws below stay inside these ranges and needn't reach their ends.
Inputs may be any that keep to these rules, and one draw needn't show every extreme that they name: `tile_values`: the matrix assembled from all used tile slots is symmetric positive definite. `tile_rows`: -1 marks an empty slot; a used slot of the device with indices (d, r) names a block row from r * 8 to (r + 1) * 8 - 1 of partition d. `tile_cols`: 0 in empty slots. `send_lists`: the 8 entries of one partition are distinct. `replace_flags`: at least one load case is flagged and at least one is not.
All inputs are finite; a program needn't handle non-finite values.
Results may differ from the reference program's by a relative error of at most 0.0003.
Values sent between devices are 32-bit elements; how exact they have to be, the bound alone decides.
A program may use at most 64 MiB of HBM per device.

```python
import jax
import jax.numpy as jnp
import numpy as np
from jax import lax

TB = 128
NC = 4
SSTEP = 3
MATCH = 6
BP_DEV = 8
GH = 4
TCAP = 64
PARTS_SIZE = 8
SPLIT = 4
BP = 32
NB = 256
TILES = 2048


COUPLING = 0.25


def hadamard_table(order_size):
    indices = np.arange(order_size)
    crossed = indices[:, None] & indices[None, :]
    parity = np.zeros((order_size, order_size), np.int64)
    for bit_index in range(max(order_size.bit_length(), 1)):
        parity = parity ^ crossed >> bit_index & 1
    return (1 - 2 * parity).astype(np.float32)


def signed_basis(sub_key):
    key_perm, key_sign = jax.random.split(sub_key)
    hadamard = jnp.asarray(hadamard_table(TB)) / jnp.sqrt(jnp.float32(TB))
    permuted = hadamard[jax.random.permutation(key_perm, TB)]
    sign_flips = jax.random.randint(key_sign, (TB,), 0, 2).astype(jnp.float32) * 2.0 - 1.0
    return permuted * sign_flips[:, None]


def layout(key):
    base_key = jax.random.fold_in(key, 4242)
    key_active, key_force, key_heavy, key_sends, key_match = jax.random.split(base_key, 5)
    active = jax.random.randint(key_active, (PARTS_SIZE,), 0, MATCH + 1)
    forced = jax.random.randint(key_force, (), 0, PARTS_SIZE)
    active = active.at[forced].set(MATCH)
    heavy_device = jax.random.randint(key_heavy, (PARTS_SIZE,), 0, SPLIT)
    heavy_device = heavy_device.at[forced].set(SPLIT - 1)
    heavy_device = heavy_device.at[(forced + 1) % PARTS_SIZE].set(0)
    shuffled = jax.vmap(lambda part_key: jax.random.permutation(part_key, BP_DEV))(jax.random.split(key_sends, PARTS_SIZE))
    send_lists = (heavy_device[:, None] * BP_DEV + shuffled[:, :2 * GH]).reshape(PARTS_SIZE, 2, GH).astype(jnp.int32)
    match_keys = jax.random.split(key_match, PARTS_SIZE * MATCH)
    pairing = jax.vmap(lambda part_key: jax.random.permutation(part_key, BP))(match_keys).reshape(PARTS_SIZE, MATCH, BP)
    return (active, heavy_device, send_lists, pairing)


def slot_tables(key):
    active, heavy_device, send_lists, pairing = layout(key)
    part_ids = jnp.arange(PARTS_SIZE)[:, None, None]
    device_ids = jnp.arange(SPLIT)[None, :, None]
    slot_ids = jnp.arange(TCAP)[None, None, :]
    inverse = jnp.argsort(pairing, axis=-1)
    slot_local = slot_ids % BP_DEV
    own_row = device_ids * BP_DEV + slot_local
    match_index = jnp.clip(slot_ids // BP_DEV - 1, 0, MATCH - 1)
    position = inverse[part_ids, match_index, own_row]
    partner = pairing[part_ids, match_index, jnp.bitwise_xor(position, 1)]
    ghost_base = BP_DEV * (1 + MATCH)
    ghost_slot = jnp.clip(slot_ids - ghost_base, 0, 2 * GH - 1)
    ghost_side = ghost_slot // GH
    ghost_index = ghost_slot % GH
    ghost_row = send_lists[part_ids, ghost_side, ghost_index]
    is_diag = slot_ids < BP_DEV
    is_match = (slot_ids >= BP_DEV) & (slot_ids < ghost_base)
    is_ghost = slot_ids >= ghost_base
    match_live = is_match & (match_index < active[part_ids])
    has_side = jnp.where(ghost_side == 0, part_ids > 0, part_ids < PARTS_SIZE - 1)
    ghost_live = is_ghost & (device_ids == heavy_device[part_ids]) & has_side
    row_table = jnp.where(is_diag | match_live, own_row, jnp.where(ghost_live, ghost_row, -1))
    col_table = jnp.where(is_diag, own_row, jnp.where(match_live, partner, jnp.where(ghost_live, BP + ghost_slot, 0)))
    slot_kind = jnp.where(is_diag, 0, jnp.where(is_match, 1, 2))
    pair_id = jnp.where(is_match, (part_ids * MATCH + match_index) * BP + position // 2, (part_ids + ghost_side) * GH + ghost_index)
    pair_id = jnp.where(is_diag, part_ids * BP + own_row, pair_id)
    flipped = jnp.where(is_match, position % 2 == 1, ghost_side == 0)
    block_ids = jnp.arange(BP)
    part_line = jnp.arange(PARTS_SIZE)
    left_hits = jnp.sum(send_lists[:, 0, :, None] == block_ids, axis=1) * (part_line > 0)[:, None]
    right_hits = jnp.sum(send_lists[:, 1, :, None] == block_ids, axis=1) * (part_line < PARTS_SIZE - 1)[:, None]
    incidence = active[:, None] + left_hits + right_hits
    shape_all = (PARTS_SIZE, SPLIT, TCAP)
    return (jnp.broadcast_to(row_table, shape_all).astype(jnp.int32), jnp.broadcast_to(col_table, shape_all).astype(jnp.int32), jnp.broadcast_to(slot_kind, shape_all).astype(jnp.int32), jnp.broadcast_to(pair_id, shape_all).astype(jnp.int32), jnp.broadcast_to(flipped, shape_all), incidence)


def draw_tile_values(key, part):
    row_table, col_table, slot_kind, pair_id, flipped, incidence = slot_tables(key)
    value_key = jax.random.fold_in(key, 777)

    def one_slot(kind_value, id_value, flip_value, incidence_value):
        sub_key = jax.random.fold_in(jax.random.fold_in(value_key, kind_value), id_value)
        key_left, key_right, key_gain, key_extra = jax.random.split(sub_key, 4)
        left_basis = signed_basis(key_left)
        right_basis = jnp.where(kind_value == 0, left_basis, signed_basis(key_right))
        gain_values = jax.random.uniform(key_gain, (TB,), jnp.float32)
        gain_values = jnp.where(kind_value == 0, 2.0 * gain_values - 1.0, 0.3 + 0.7 * gain_values)
        tile_value = COUPLING * jnp.dot(left_basis * gain_values[None, :], right_basis.T, precision=lax.Precision.HIGHEST)
        tile_value = jnp.where(flip_value, tile_value.T, tile_value)
        extra_diag = jnp.exp(jax.random.uniform(key_extra, (TB,), jnp.float32, jnp.log(0.05), jnp.log(0.5)))
        diagonal = COUPLING * (incidence_value + 1.0) + extra_diag
        return tile_value + jnp.where(kind_value == 0, 1.0, 0.0) * jnp.diag(diagonal)

    def one_part(packed):
        part_kind, part_id, part_flip, part_rows, part_incidence = packed
        slot_incidence = part_incidence[jnp.clip(part_rows, 0, BP - 1)].astype(jnp.float32)
        return jax.vmap(one_slot)(part_kind, part_id, part_flip, slot_incidence)
    tile_stack = lax.map(one_part, (slot_kind.reshape(PARTS_SIZE, SPLIT * TCAP), pair_id.reshape(PARTS_SIZE, SPLIT * TCAP), flipped.reshape(PARTS_SIZE, SPLIT * TCAP), row_table.reshape(PARTS_SIZE, SPLIT * TCAP), incidence))
    return tile_stack.reshape(TILES, TB, TB)


def draw_tile_rows(key, part):
    return slot_tables(key)[0].reshape(TILES)


def draw_tile_cols(key, part):
    return slot_tables(key)[1].reshape(TILES)


def draw_send_lists(key, part):
    return layout(key)[2]


def draw_replace_flags(key, part):
    flag_key = jax.random.fold_in(key, 31)
    key_perm, key_count = jax.random.split(flag_key)
    ranking = jax.random.permutation(key_perm, NC)
    flagged_count = jax.random.randint(key_count, (), 1, NC)
    return (ranking < flagged_count).astype(jnp.int32)


def vector_draw(key, salt):
    sub_key = jax.random.fold_in(key, salt)
    key_noise, key_scale = jax.random.split(sub_key, 2)
    part_ramp = 1.0 + 2.0 * jnp.arange(PARTS_SIZE, dtype=jnp.float32) / max(PARTS_SIZE - 1, 1)
    block_ramp = jnp.repeat(part_ramp, BP)
    row_scale = jnp.exp(jax.random.uniform(key_scale, (NC, NB, 1), jnp.float32, jnp.log(0.4), jnp.log(1.2)))
    row_scale = row_scale * block_ramp[None, :, None]
    noise_part = jax.random.normal(key_noise, (NC, NB, TB), jnp.float32)
    return row_scale * noise_part


def draw_right_side(key, part):
    return vector_draw(key, 11)


def draw_start_iterate(key, part):
    return vector_draw(key, 12)


def draw_start_residual(key, part):
    return vector_draw(key, 13)


def draw_start_direction(key, part):
    return vector_draw(key, 14)


def setup_inputs(seed: int = 0) -> dict:
    key_list = jax.random.split(jax.random.key(seed), 10)
    tile_values = draw_tile_values(jax.random.fold_in(key_list[9], 71), 0)
    tile_rows = draw_tile_rows(jax.random.fold_in(key_list[9], 71), 0)
    tile_cols = draw_tile_cols(jax.random.fold_in(key_list[9], 71), 0)
    send_lists = draw_send_lists(jax.random.fold_in(key_list[9], 71), 0)
    replace_flags = draw_replace_flags(jax.random.fold_in(key_list[9], 71), 0)
    right_side = draw_right_side(jax.random.fold_in(key_list[9], 71), 0)
    start_iterate = draw_start_iterate(jax.random.fold_in(key_list[9], 71), 0)
    start_residual = draw_start_residual(jax.random.fold_in(key_list[9], 71), 0)
    start_direction = draw_start_direction(jax.random.fold_in(key_list[9], 71), 0)
    return dict(tile_values=tile_values, tile_rows=tile_rows, tile_cols=tile_cols, send_lists=send_lists, replace_flags=replace_flags, right_side=right_side, start_iterate=start_iterate, start_residual=start_residual, start_direction=start_direction)


highest = lax.Precision.HIGHEST


def shift_table(basis_steps):
    basis_width = 2 * basis_steps + 1
    shift_matrix = np.zeros((basis_width, basis_width), np.float32)
    for position in range(basis_steps):
        shift_matrix[position + 1, position] = 1.0
    for position in range(basis_steps - 1):
        shift_matrix[basis_steps + 2 + position, basis_steps + 1 + position] = 1.0
    return shift_matrix


def coefficients(gram_matrix, basis_steps):
    shift_matrix = jnp.asarray(shift_table(basis_steps))
    case_count = gram_matrix.shape[0]
    basis_width = gram_matrix.shape[1]
    eye_matrix = jnp.eye(basis_width, dtype=jnp.float32)
    direction = jnp.broadcast_to(eye_matrix[0], (case_count, basis_width))
    residual = jnp.broadcast_to(eye_matrix[basis_steps + 1], (case_count, basis_width))
    iterate = jnp.zeros((case_count, basis_width), jnp.float32)

    def quadratic(first_vec, second_vec):
        return jnp.einsum('ci,cij,cj->c', first_vec, gram_matrix, second_vec, precision=highest)

    res_norm = quadratic(residual, residual)
    for inner_step in range(basis_steps):
        mapped = jnp.einsum('ij,cj->ci', shift_matrix, direction, precision=highest)
        step_size = res_norm / quadratic(direction, mapped)
        iterate = iterate + step_size[:, None] * direction
        residual = residual - step_size[:, None] * mapped
        next_norm = quadratic(residual, residual)
        direction = residual + (next_norm / res_norm)[:, None] * direction
        res_norm = next_norm
    return iterate, residual, direction


def combine(basis_stack, weights):
    return jnp.einsum('icbt,ci->cbt', basis_stack, weights, precision=highest)


def spread_ghosts(blocks, send_lists):
    flat_sends = send_lists.reshape(PARTS_SIZE, 2 * GH)
    picked = jax.vmap(lambda part_blocks, part_sends: jnp.take(part_blocks, part_sends, axis=2),
                      in_axes=(2, 0), out_axes=2)(blocks, flat_sends)
    to_left = picked[:, :, :, :GH]
    to_right = picked[:, :, :, GH:]
    zero_part = jnp.zeros_like(to_left[:, :, :1])
    from_left = jnp.concatenate([zero_part, to_right[:, :, :-1]], axis=2)
    from_right = jnp.concatenate([to_left[:, :, 1:], zero_part], axis=2)
    return jnp.concatenate([blocks, from_left, from_right], axis=3)


def apply_matrix(vectors, tile_values, tile_rows, tile_cols, send_lists):
    stack_count = vectors.shape[0]
    blocks = vectors.reshape(stack_count, NC, PARTS_SIZE, BP, TB)
    extended = spread_ghosts(blocks, send_lists)
    part_tiles = tile_values.reshape(PARTS_SIZE, SPLIT * TCAP, TB, TB)
    part_rows = tile_rows.reshape(PARTS_SIZE, SPLIT * TCAP)
    part_cols = tile_cols.reshape(PARTS_SIZE, SPLIT * TCAP)

    def one_part(packed):
        ext_part, tile_part, row_part, col_part = packed
        picked = jnp.take(ext_part, col_part, axis=2)
        product = jnp.einsum('tij,kctj->kcti', tile_part, picked, precision=highest)
        wanted = lax.iota(jnp.int32, BP)
        onehot = (row_part[:, None] == wanted[None, :]).astype(jnp.float32)
        return jnp.einsum('tb,kcti->kcbi', onehot, product, precision=highest)

    result = lax.map(one_part, (jnp.moveaxis(extended, 2, 0), part_tiles, part_rows, part_cols))
    return jnp.moveaxis(result, 0, 2).reshape(stack_count, NC, NB, TB)


def basis_from(apply_operator, direction, residual):
    direction_powers = [direction]
    residual_powers = [residual]
    for power_step in range(SSTEP):
        members = [direction_powers[-1]]
        if power_step < SSTEP - 1:
            members.append(residual_powers[-1])
        mapped = apply_operator(jnp.stack(members))
        direction_powers.append(mapped[0])
        if power_step < SSTEP - 1:
            residual_powers.append(mapped[1])
    return jnp.stack(direction_powers + residual_powers)


def reference(tile_values, tile_rows, tile_cols, send_lists, replace_flags, right_side, start_iterate, start_residual, start_direction):
    def apply_operator(vectors):
        return apply_matrix(vectors, tile_values, tile_rows, tile_cols, send_lists)

    basis_stack = basis_from(apply_operator, start_direction, start_residual)
    gram_matrix = jnp.einsum('icbt,jcbt->cij', basis_stack, basis_stack, precision=highest)
    iterate_coef, residual_coef, direction_coef = coefficients(gram_matrix, SSTEP)
    new_iterate = start_iterate + combine(basis_stack, iterate_coef)
    recursive = combine(basis_stack, residual_coef)
    new_direction = combine(basis_stack, direction_coef)
    replaced = right_side - apply_operator(new_iterate[None])[0]
    new_residual = jnp.where(replace_flags[:, None, None] > 0, replaced, recursive)
    return new_iterate, new_residual, new_direction
```

```python
import functools

import jax
import jax.numpy as jnp
from jax import lax
from jax.experimental import pallas as pl
from jax.experimental.pallas import tpu as pltpu
from jax.sharding import PartitionSpec as P

SSTEP = 3
WIDTH = 2 * SSTEP + 1
P0, R0, X0, P1, R1, P2 = range(6)
SENT = 6
MESH = pl.DeviceIdType.MESH
UNROLL = 16


def moment_of(i, j):
    sides = (i > SSTEP) + (j > SSTEP)
    return sides, i + j - sides * (SSTEP + 1)


PAIRS = [(i, j) for i in range(WIDTH) for j in range(i, WIDTH)]
MOMENTS = sorted({moment_of(i, j) for i, j in PAIRS})
ENTRY = {moment: e for e, moment in enumerate(MOMENTS)}


def shifted_of(vec):
    return {i + 1: v for i, v in vec.items() if i not in (SSTEP, WIDTH - 1)}


def axpy(base, scale, other, sign):
    out = dict(base)
    for i, v in other.items():
        term = scale * v
        if i in out:
            out[i] = out[i] + term if sign > 0 else out[i] - term
        else:
            out[i] = term if sign > 0 else -term
    return out


def coefficients(gram):
    def quadratic(first, second):
        total = None
        for i, a in first.items():
            inner = None
            for j, b in second.items():
                term = gram[(min(i, j), max(i, j))] * b
                inner = term if inner is None else inner + term
            inner = inner * a
            total = inner if total is None else total + inner
        return total

    one = jnp.ones_like(gram[(0, 0)])
    direction = {0: one}
    residual = {SSTEP + 1: one}
    iterate = {}
    norm = quadratic(residual, residual)
    for _ in range(SSTEP):
        mapped = shifted_of(direction)
        step = norm / quadratic(direction, mapped)
        iterate = axpy(iterate, step, direction, 1)
        residual = axpy(residual, step, mapped, -1)
        next_norm = quadratic(residual, residual)
        direction = axpy(residual, next_norm / norm, direction, 1)
        norm = next_norm
    return iterate, residual, direction


def kernel(
    parts,
    split,
    rows_h,
    cols_h,
    sends_h,
    flags_h,
    tiles_h,
    direction_h,
    residual_h,
    iterate_h,
    right_h,
    out_ref,
    *scratch,
):
    scratch = list(scratch)
    take = lambda n: [scratch.pop(0) for _ in range(n)]
    ext = take(SENT)
    own = take(SENT + 3)
    ghost_send = take(SENT)
    ghost_recv = take(SENT)
    tiles, weights, vec_in, gram_own, gram_all = take(5)
    rows_s, cols_s, sends_s, flags_s = take(4)
    tile_sem, vec_sem, index_sem, peer_send, peer_recv, side_send, side_recv = take(7)
    gram_send, gram_recv = take(2)

    d, r = lax.axis_index("dom"), lax.axis_index("rhs")
    cases, own_rows, tb = own[0].shape[1], own[0].shape[0], own[0].shape[2]
    gh = ghost_send[0].shape[1]
    tile_count = tiles.shape[0]
    chunks = tile_sem.shape[0]
    per_chunk = tile_count // chunks
    base = r * own_rows
    me = d * split + r
    has_left, has_right = d > 0, d < parts - 1
    core_count = 2 if split % 2 == 0 else 1
    chips = split // core_count
    others = []
    for h in range(1, chips):
        for c in range(core_count):
            chip = lax.rem(r // core_count + h, chips)
            others.append(chip * core_count + lax.rem(r + c, core_count))
    others += [
        r // core_count * core_count + lax.rem(r + c, core_count)
        for c in range(1, core_count)
    ]

    def far_first(k):
        down = parts - k - (parts - k <= d).astype(jnp.int32)
        up = k - 1 + (k - 1 >= d).astype(jnp.int32)
        return jnp.where(2 * d < parts, down, up)

    barrier = pltpu.get_barrier_semaphore()

    def greet(dd, rr):
        pl.semaphore_signal(barrier, inc=1, device_id=(dd, rr), device_id_type=MESH)

    @pl.loop(1, parts)
    def _(k):
        to = far_first(k)
        for rr in others + [r]:
            greet(to, rr)

    for rr in others:
        greet(d, rr)

    vec_copies = [
        pltpu.make_async_copy(ref, vec_in.at[i], vec_sem.at[i])
        for i, ref in enumerate((direction_h, residual_h, iterate_h, right_h))
    ]
    index_copies = [
        pltpu.make_async_copy(ref, to, index_sem.at[i])
        for i, (ref, to) in enumerate(
            ((sends_h, sends_s), (cols_h, cols_s), (rows_h, rows_s), (flags_h, flags_s))
        )
    ]
    vec_copies[0].start()
    index_copies[0].start()
    vec_copies[1].start()
    tile_copies = []
    for i in range(chunks):
        part = pl.ds(i * per_chunk, per_chunk)
        copy = pltpu.make_async_copy(tiles_h.at[part], tiles.at[part], tile_sem.at[i])
        copy.start()
        tile_copies.append(copy)
    for copy in vec_copies[2:] + index_copies[1:]:
        copy.start()

    first_ghost = split * own_rows
    for v in range(SENT):
        ext[v][pl.ds(first_ghost, 2 * gh)] = jnp.zeros((2 * gh, cases, tb), jnp.float32)

    def peer_copy(v, to):
        return pltpu.make_async_remote_copy(
            src_ref=own[v],
            dst_ref=ext[v].at[pl.ds(base, own_rows)],
            send_sem=peer_send.at[v],
            recv_sem=peer_recv.at[v],
            device_id=(d, to),
            device_id_type=MESH,
        )

    def side_copy(v, side, to):
        return pltpu.make_async_remote_copy(
            src_ref=ghost_send[v].at[side],
            dst_ref=ghost_recv[v].at[1 - side, r],
            send_sem=side_send.at[v, side],
            recv_sem=side_recv.at[v, 1 - side],
            device_id=(d - 1 + 2 * side, to),
            device_id_type=MESH,
        )

    def arrived(ref, sem):
        pltpu.make_async_copy(ref, ref, sem).wait()

    def stage(v, values):
        for b in range(own_rows):
            own[v][b] = values[b]
            ext[v][base + b] = values[b]
        for side in range(2):
            for k in range(gh):
                local = sends_s[0, side, k] - base
                value = own[v][jnp.clip(local, 0, own_rows - 1)]
                where = jnp.full((cases, tb), local, jnp.int32)
                ghost_send[v][side, k] = jnp.where(
                    (where >= 0) & (where < own_rows), value, 0.0
                )

    early_side = lax.rem(d, 2)

    def send(v):
        for side in (early_side, 1 - early_side):

            @pl.when(jnp.where(side == 0, has_left, has_right))
            def _():
                for to in others + [r]:
                    side_copy(v, side, to).start()

        for to in others:
            peer_copy(v, to).start()

    def receive(v):
        arrived(ext[v].at[pl.ds(0, (split - 1) * own_rows)], peer_recv.at[v])
        for side, present in ((0, has_left), (1, has_right)):

            @pl.when(present)
            def _():
                arrived(ghost_recv[v].at[side], side_recv.at[v, side])
                total = ghost_recv[v][side, 0]
                for o in range(1, split):
                    total = total + ghost_recv[v][side, o]
                ext[v][pl.ds(first_ghost + side * gh, gh)] = total

    def sent(v):
        arrived(ext[v].at[pl.ds(0, (split - 1) * own_rows)], peer_send.at[v])
        for side, present in ((0, has_left), (1, has_right)):

            @pl.when(present)
            def _():
                arrived(ghost_recv[v].at[side], side_send.at[v, side])

    def input_blocks(i):
        return [vec_in[i, :, b, :] for b in range(own_rows)]

    low = lax.broadcasted_iota(jnp.int32, (2 * cases, tb), 0) < cases

    def apply_to(v):
        def step(i, acc):
            acc = list(acc)
            for u in range(UNROLL):
                q = i * UNROLL + u
                pair = jnp.concatenate(
                    [ext[v][cols_s[2 * q]], ext[v][cols_s[2 * q + 1]]], axis=0
                )
                high = pair.astype(jnp.bfloat16).astype(jnp.float32)
                lhs = jnp.concatenate([high, pair - high], axis=0).astype(jnp.bfloat16)
                lhs = jnp.concatenate([lhs, lhs], axis=1)
                out = jnp.dot(lhs, weights[q], preferred_element_type=jnp.float32)
                out = out[: 2 * cases] + out[2 * cases :]
                out = jnp.where(low, out[:, :tb], out[:, tb:])
                row = jnp.where(low, rows_s[2 * q], rows_s[2 * q + 1]) - base
                acc = [a + jnp.where(row == b, out, 0.0) for b, a in enumerate(acc)]
            return tuple(acc)

        zero = jnp.zeros((2 * cases, tb), jnp.float32)
        acc = lax.fori_loop(0, tile_count // 2 // UNROLL, step, (zero,) * own_rows)
        return [a[:cases] + a[cases:] for a in acc]

    index_copies[0].wait()
    for v in range(2):
        vec_copies[v].wait()
        stage(v, input_blocks(v))
    pl.semaphore_wait(barrier, parts * split - 1)
    send(P0)
    send(R0)
    for copy in vec_copies[2:] + index_copies[1:]:
        copy.wait()
    stage(X0, input_blocks(X0))

    for i in range(chunks):
        tile_copies[i].wait()

        @pl.loop(i * per_chunk // 2, (i + 1) * per_chunk // 2)
        def _(q):
            for h in range(2):
                flipped = tiles[2 * q + h].T
                high = flipped.astype(jnp.bfloat16)
                weights[q, :tb, h * tb : (h + 1) * tb] = high
                weights[q, tb:, h * tb : (h + 1) * tb] = (
                    flipped - high.astype(jnp.float32)
                ).astype(jnp.bfloat16)

    case_of = lax.broadcasted_iota(jnp.int32, (cases, tb), 0)
    entry_of = lax.broadcasted_iota(jnp.int32, (cases, tb), 1) - case_of
    basis = [own[P0], own[P1], own[P2], own[SENT], own[R0], own[R1], own[SENT + 1]]
    image = own[SENT + 2]
    done = set()

    def gram_of(payload, known):
        for i, j in PAIRS:
            moment = moment_of(i, j)
            if moment in done or i not in known or j not in known:
                continue
            if abs(i - j) > 1 and moment[0] != 1:
                continue
            done.add(moment)
            total = basis[i][0] * basis[j][0]
            for b in range(1, own_rows):
                total = total + basis[i][b] * basis[j][b]
            total = jnp.sum(total, axis=1, keepdims=True)
            payload = payload + jnp.where(entry_of == cases * ENTRY[moment], total, 0.0)
        return payload

    receive(P0)
    stage(P1, apply_to(P0))
    send(P1)
    receive(R0)
    stage(R1, apply_to(R0))
    send(R1)
    send(X0)
    payload = jnp.zeros((cases, tb), jnp.float32)
    payload = gram_of(payload, (0, 1, 4, 5))
    receive(P1)
    stage(P2, apply_to(P1))
    send(P2)
    receive(R1)
    for b, value in enumerate(apply_to(R1)):
        own[SENT + 1][b] = value
    payload = gram_of(payload, (0, 1, 2, 4, 5, 6))
    receive(X0)
    flag = jnp.zeros((cases, tb), jnp.int32)
    for c in range(cases):
        flag = jnp.where(case_of == c, flags_s[c], flag)
    flagged = flag > 0
    for b, value in enumerate(apply_to(X0)):
        image[b] = jnp.where(flagged, vec_in[3, :, b, :] - value, 0.0)
    receive(P2)
    for b, value in enumerate(apply_to(P2)):
        own[SENT][b] = value
    payload = gram_of(payload, range(WIDTH))
    assert len(done) == len(MOMENTS)

    payload = jnp.sum(payload, axis=0, keepdims=True)
    gram_own[0] = payload
    gram_all[me] = payload

    def gram_copy(dd, rr):
        return pltpu.make_async_remote_copy(
            src_ref=gram_own.at[0],
            dst_ref=gram_all.at[me],
            send_sem=gram_send,
            recv_sem=gram_recv,
            device_id=(dd, rr),
            device_id_type=MESH,
        )

    @pl.loop(1, parts)
    def _(k):
        to = far_first(k)
        for rr in others + [r]:
            gram_copy(to, rr).start()

    for rr in others:
        gram_copy(d, rr).start()

    for v in range(SENT):
        sent(v)

    foreign = gram_all.at[pl.ds(0, parts * split - 1)]
    arrived(foreign, gram_send)
    arrived(foreign, gram_recv)

    whole = jnp.broadcast_to(jnp.sum(gram_all[...], axis=0), (cases, tb))
    entries = [
        jnp.broadcast_to(
            jnp.sum(jnp.where(entry_of == cases * e, whole, 0.0), axis=1, keepdims=True),
            (cases, tb),
        )
        for e in range(len(MOMENTS))
    ]
    gram = {pair: entries[ENTRY[moment_of(*pair)]] for pair in PAIRS}
    iterate_c, residual_c, direction_c = coefficients(gram)
    shifted_c = shifted_of(iterate_c)
    replace_c = {
        i: jnp.where(flagged, -shifted_c[i], w) if i in shifted_c else jnp.where(flagged, 0.0, w)
        for i, w in residual_c.items()
    }
    for b in range(own_rows):
        blocks = [ref[b] for ref in basis]

        def combine(total, weights_of):
            for i, w in weights_of.items():
                total = blocks[i] * w if total is None else total + blocks[i] * w
            return total

        out_ref[0, :, b, :] = combine(vec_in[2, :, b, :], iterate_c)
        out_ref[1, :, b, :] = combine(image[b], replace_c)
        out_ref[2, :, b, :] = combine(None, direction_c)


def write_out(made_ref, *refs):
    outs, sem = refs[:-1], refs[-1]
    copies = [
        pltpu.make_async_copy(made_ref.at[i], ref, sem.at[i]) for i, ref in enumerate(outs)
    ]
    for copy in copies:
        copy.start()
    for copy in copies:
        copy.wait()


def body(parts, split, tiles, rows, cols, sends, flags, right, iterate, residual, direction):
    cases, own_rows, tb = residual.shape
    gh = sends.shape[2]
    count = tiles.shape[0]
    f32 = jnp.float32
    dma = pltpu.SemaphoreType.DMA
    hbm = pl.BlockSpec(memory_space=pltpu.HBM)
    vmem = pl.BlockSpec(memory_space=pltpu.VMEM)
    scratch = (
        [pltpu.VMEM((split * own_rows + 2 * gh, cases, tb), f32)] * SENT
        + [pltpu.VMEM((own_rows, cases, tb), f32)] * (SENT + 3)
        + [pltpu.VMEM((2, gh, cases, tb), f32)] * SENT
        + [pltpu.VMEM((2, split, gh, cases, tb), f32)] * SENT
        + [
            pltpu.VMEM((count, tb, tb), f32),
            pltpu.VMEM((count // 2, 2 * tb, 2 * tb), jnp.bfloat16),
            pltpu.VMEM((4, cases, own_rows, tb), f32),
            pltpu.VMEM((1, 1, tb), f32),
            pltpu.VMEM((parts * split, 1, tb), f32),
            pltpu.SMEM(rows.shape, jnp.int32),
            pltpu.SMEM(cols.shape, jnp.int32),
            pltpu.SMEM(sends.shape, jnp.int32),
            pltpu.SMEM(flags.shape, jnp.int32),
            dma((4,)),
            dma((4,)),
            dma((4,)),
            dma((SENT,)),
            dma((SENT,)),
            dma((SENT, 2)),
            dma((SENT, 2)),
            dma,
            dma,
        ]
    )
    made = pl.pallas_call(
        functools.partial(kernel, parts, split),
        out_shape=pltpu.VMEM((3, cases, own_rows, tb), f32),
        in_specs=[hbm] * 9,
        out_specs=vmem,
        scratch_shapes=scratch,
        compiler_params=pltpu.CompilerParams(
            collective_id=0, has_side_effects=True, vmem_limit_bytes=63 * 1024 * 1024
        ),
    )(rows, cols, sends, flags, tiles, direction, residual, iterate, right)
    return pl.pallas_call(
        write_out,
        out_shape=[jax.ShapeDtypeStruct(residual.shape, f32)] * 3,
        in_specs=[vmem],
        out_specs=[hbm] * 3,
        scratch_shapes=[dma((3,))],
    )(pltpu.with_memory_space_constraint(made, pltpu.VMEM))


def solution(mesh):
    both = ("dom", "rhs")
    vec = P(None, both, None)
    placed = (P(both, None, None), P(both), P(both), P("dom", None, None), P(), vec, vec, vec, vec)
    return jax.shard_map(
        functools.partial(body, mesh.shape["dom"], mesh.shape["rhs"]),
        mesh=mesh,
        in_specs=placed,
        out_specs=(vec, vec, vec),
        check_vma=False,
    )
```

```python
import functools

import jax
import jax.numpy as jnp
from jax import lax
from jax.experimental import pallas as pl
from jax.experimental.pallas import tpu as pltpu
from jax.sharding import PartitionSpec as P

SSTEP = 3
WIDTH = 2 * SSTEP + 1
P0, P1, P2, R1, R0, X0 = range(6)
WIDE = 4
SENT = 6
MESH = pl.DeviceIdType.MESH
UNROLL = 16


def moment_of(i, j):
    sides = (i > SSTEP) + (j > SSTEP)
    return sides, i + j - sides * (SSTEP + 1)


PAIRS = [(i, j) for i in range(WIDTH) for j in range(i, WIDTH)]
MOMENTS = sorted({moment_of(i, j) for i, j in PAIRS})
ENTRY = {moment: e for e, moment in enumerate(MOMENTS)}


def shifted_of(vec):
    return {i + 1: v for i, v in vec.items() if i not in (SSTEP, WIDTH - 1)}


def axpy(base, scale, other, sign):
    out = dict(base)
    for i, v in other.items():
        term = scale * v
        if i in out:
            out[i] = out[i] + term if sign > 0 else out[i] - term
        else:
            out[i] = term if sign > 0 else -term
    return out


def coefficients(gram):
    def quadratic(first, second):
        total = None
        for i, a in first.items():
            inner = None
            for j, b in second.items():
                term = gram[(min(i, j), max(i, j))] * b
                inner = term if inner is None else inner + term
            inner = inner * a
            total = inner if total is None else total + inner
        return total

    one = jnp.ones_like(gram[(0, 0)])
    direction = {0: one}
    residual = {SSTEP + 1: one}
    iterate = {}
    norm = quadratic(residual, residual)
    for _ in range(SSTEP):
        mapped = shifted_of(direction)
        step = norm / quadratic(direction, mapped)
        iterate = axpy(iterate, step, direction, 1)
        residual = axpy(residual, step, mapped, -1)
        next_norm = quadratic(residual, residual)
        direction = axpy(residual, next_norm / norm, direction, 1)
        norm = next_norm
    return iterate, residual, direction


def kernel(
    parts,
    split,
    rows_h,
    cols_h,
    sends_h,
    flags_h,
    tiles_h,
    direction_h,
    residual_h,
    iterate_h,
    right_h,
    out_ref,
    *scratch,
):
    scratch = list(scratch)
    take = lambda n: [scratch.pop(0) for _ in range(n)]
    ext = take(SENT)
    own = take(SENT + 3)
    ghost_send = take(SENT)
    ghost_recv = take(WIDE)
    line_recv = take(SENT - WIDE)
    tiles, weights, vec_in, gram_own, gram_all = take(5)
    rows_s, cols_s, sends_s, flags_s = take(4)
    tile_sem, vec_sem, index_sem, peer_send, peer_recv, side_send, side_recv = take(7)
    gram_send, gram_recv = take(2)

    d, r = lax.axis_index("dom"), lax.axis_index("rhs")
    cases, own_rows, tb = own[0].shape[1], own[0].shape[0], own[0].shape[2]
    gh = ghost_send[0].shape[1]
    tile_count = tiles.shape[0]
    chunks = tile_sem.shape[0]
    per_chunk = tile_count // chunks
    base = r * own_rows
    me = d * split + r
    has_left, has_right = d > 0, d < parts - 1
    core_count = 2 if split % 2 == 0 else 1
    chips = split // core_count
    others = []
    for h in range(1, chips):
        for c in range(core_count):
            chip = lax.rem(r // core_count + h, chips)
            others.append(chip * core_count + lax.rem(r + c, core_count))
    others += [
        r // core_count * core_count + lax.rem(r + c, core_count)
        for c in range(1, core_count)
    ]

    def far_first(k):
        down = parts - k - (parts - k <= d).astype(jnp.int32)
        up = k - 1 + (k - 1 >= d).astype(jnp.int32)
        return jnp.where(2 * d < parts, down, up)

    barrier = pltpu.get_barrier_semaphore()

    def greet(dd, rr):
        pl.semaphore_signal(barrier, inc=1, device_id=(dd, rr), device_id_type=MESH)

    @pl.loop(1, parts)
    def _(k):
        to = far_first(k)
        for rr in others + [r]:
            greet(to, rr)

    for rr in others:
        greet(d, rr)

    vec_copies = [
        pltpu.make_async_copy(ref, vec_in.at[i], vec_sem.at[i])
        for i, ref in enumerate((direction_h, residual_h, iterate_h, right_h))
    ]
    index_copies = [
        pltpu.make_async_copy(ref, to, index_sem.at[i])
        for i, (ref, to) in enumerate(
            ((sends_h, sends_s), (cols_h, cols_s), (rows_h, rows_s), (flags_h, flags_s))
        )
    ]
    vec_copies[0].start()
    index_copies[0].start()
    vec_copies[1].start()
    vec_copies[2].start()
    tile_copies = []
    for i in range(chunks):
        part = pl.ds(i * per_chunk, per_chunk)
        copy = pltpu.make_async_copy(tiles_h.at[part], tiles.at[part], tile_sem.at[i])
        copy.start()
        tile_copies.append(copy)
    for copy in vec_copies[3:] + index_copies[1:]:
        copy.start()

    first_ghost = split * own_rows
    for v in range(SENT):
        ext[v][pl.ds(first_ghost, 2 * gh)] = jnp.zeros((2 * gh, cases, tb), jnp.float32)

    def peer_copy(v, to):
        return pltpu.make_async_remote_copy(
            src_ref=own[v],
            dst_ref=ext[v].at[pl.ds(base, own_rows)],
            send_sem=peer_send.at[v],
            recv_sem=peer_recv.at[v],
            device_id=(d, to),
            device_id_type=MESH,
        )

    def side_copy(v, side, to):
        return pltpu.make_async_remote_copy(
            src_ref=ghost_send[v].at[side],
            dst_ref=ghost_recv[v].at[1 - side, r],
            send_sem=side_send.at[v, side],
            recv_sem=side_recv.at[v, 1 - side],
            device_id=(d - 1 + 2 * side, to),
            device_id_type=MESH,
        )

    def arrived(ref, sem):
        pltpu.make_async_copy(ref, ref, sem).wait()

    def keep(v, values):
        for b in range(own_rows):
            own[v][b] = values[b]
            ext[v][base + b] = values[b]

    def stage(v, values):
        keep(v, values)
        for side in range(2):
            for k in range(gh):
                local = sends_s[0, side, k] - base
                value = own[v][jnp.clip(local, 0, own_rows - 1)]
                where = jnp.full((cases, tb), local, jnp.int32)
                ghost_send[v][side, k] = jnp.where(
                    (where >= 0) & (where < own_rows), value, 0.0
                )

    early_side = lax.rem(d, 2)

    def send(v):
        for side in (early_side, 1 - early_side):

            @pl.when(jnp.where(side == 0, has_left, has_right))
            def _():
                for to in others + [r]:
                    side_copy(v, side, to).start()

        send_peers(v)

    def send_peers(v):
        for to in others:
            peer_copy(v, to).start()

    def receive_peers(v):
        arrived(ext[v].at[pl.ds(0, (split - 1) * own_rows)], peer_recv.at[v])

    def line_copy(v, side):
        return pltpu.make_async_remote_copy(
            src_ref=ghost_send[v].at[side],
            dst_ref=line_recv[v - WIDE].at[1 - side],
            send_sem=side_send.at[v, side],
            recv_sem=side_recv.at[v, 1 - side],
            device_id=(d - 1 + 2 * side, r),
            device_id_type=MESH,
        )

    def send_line(v):
        for side in range(2):
            for k in range(gh):
                ghost_send[v][side, k] = ext[v][sends_s[0, side, k]]
        for side, present in ((0, has_left), (1, has_right)):

            @pl.when(present)
            def _():
                line_copy(v, side).start()

    def receive_line(v):
        for side, present in ((0, has_left), (1, has_right)):

            @pl.when(present)
            def _():
                arrived(line_recv[v - WIDE].at[side], side_recv.at[v, side])
                ext[v][pl.ds(first_ghost + side * gh, gh)] = line_recv[v - WIDE][side]

    def receive(v):
        receive_peers(v)
        for side, present in ((0, has_left), (1, has_right)):

            @pl.when(present)
            def _():
                arrived(ghost_recv[v].at[side], side_recv.at[v, side])
                total = ghost_recv[v][side, 0]
                for o in range(1, split):
                    total = total + ghost_recv[v][side, o]
                ext[v][pl.ds(first_ghost + side * gh, gh)] = total

    def sent(v):
        arrived(ext[v].at[pl.ds(0, (split - 1) * own_rows)], peer_send.at[v])
        for side, present in ((0, has_left), (1, has_right)):

            @pl.when(present)
            def _():
                arrived(
                    ghost_recv[v].at[side] if v < WIDE else ghost_send[v].at[side],
                    side_send.at[v, side],
                )

    def input_blocks(i):
        return [vec_in[i, :, b, :] for b in range(own_rows)]

    low = lax.broadcasted_iota(jnp.int32, (2 * cases, tb), 0) < cases

    def apply_to(*vs):
        def step(i, accs):
            accs = list(accs)
            for u in range(UNROLL):
                q = i * UNROLL + u
                lhs = []
                for v in vs:
                    pair = jnp.concatenate(
                        [ext[v][cols_s[2 * q]], ext[v][cols_s[2 * q + 1]]], axis=0
                    )
                    high = pair.astype(jnp.bfloat16).astype(jnp.float32)
                    lhs += [high, pair - high]
                lhs = jnp.concatenate(lhs, axis=0).astype(jnp.bfloat16)
                lhs = jnp.concatenate([lhs, lhs], axis=1)
                out = jnp.dot(lhs, weights[q], preferred_element_type=jnp.float32)
                row = jnp.where(low, rows_s[2 * q], rows_s[2 * q + 1]) - base
                for n in range(len(vs)):
                    part = out[4 * cases * n : 4 * cases * (n + 1)]
                    part = part[: 2 * cases] + part[2 * cases :]
                    part = jnp.where(low, part[:, :tb], part[:, tb:])
                    for b in range(own_rows):
                        k = n * own_rows + b
                        accs[k] = accs[k] + jnp.where(row == b, part, 0.0)
            return tuple(accs)

        zero = jnp.zeros((2 * cases, tb), jnp.float32)
        accs = (zero,) * (own_rows * len(vs))
        accs = lax.fori_loop(0, tile_count // 2 // UNROLL, step, accs)
        sums = [a[:cases] + a[cases:] for a in accs]
        return [sums[n * own_rows : (n + 1) * own_rows] for n in range(len(vs))]

    index_copies[0].wait()
    vec_copies[0].wait()
    stage(P0, input_blocks(0))
    for i, v in ((1, R0), (2, X0)):
        vec_copies[i].wait()
        keep(v, input_blocks(i))
    pl.semaphore_wait(barrier, parts * split - 1)
    send(P0)
    send_peers(R0)
    for copy in vec_copies[3:] + index_copies[1:]:
        copy.wait()

    for i in range(chunks):
        tile_copies[i].wait()

        @pl.loop(i * per_chunk // 2, (i + 1) * per_chunk // 2)
        def _(q):
            for h in range(2):
                flipped = tiles[2 * q + h].T
                high = flipped.astype(jnp.bfloat16)
                weights[q, :tb, h * tb : (h + 1) * tb] = high
                weights[q, tb:, h * tb : (h + 1) * tb] = (
                    flipped - high.astype(jnp.float32)
                ).astype(jnp.bfloat16)

    case_of = lax.broadcasted_iota(jnp.int32, (cases, tb), 0)
    entry_of = lax.broadcasted_iota(jnp.int32, (cases, tb), 1) - case_of
    basis = [own[P0], own[P1], own[P2], own[SENT], own[R0], own[R1], own[SENT + 1]]
    image = own[SENT + 2]
    done = set()

    def gram_of(payload, known):
        for i, j in PAIRS:
            moment = moment_of(i, j)
            if moment in done or i not in known or j not in known:
                continue
            if abs(i - j) > 1 and moment[0] != 1:
                continue
            done.add(moment)
            total = basis[i][0] * basis[j][0]
            for b in range(1, own_rows):
                total = total + basis[i][b] * basis[j][b]
            total = jnp.sum(total, axis=1, keepdims=True)
            payload = payload + jnp.where(entry_of == cases * ENTRY[moment], total, 0.0)
        return payload

    receive_peers(R0)
    send_line(R0)
    receive(P0)
    stage(P1, apply_to(P0)[0])
    send(P1)
    send_peers(X0)
    flag = jnp.zeros((cases, tb), jnp.int32)
    for c in range(cases):
        flag = jnp.where(case_of == c, flags_s[c], flag)
    flagged = flag > 0
    receive_line(R0)
    stage(R1, apply_to(R0)[0])
    send(R1)
    payload = jnp.zeros((cases, tb), jnp.float32)
    payload = gram_of(payload, (0, 1, 4, 5))
    receive_peers(X0)
    send_line(X0)
    receive(P1)
    stage(P2, apply_to(P1)[0])
    send(P2)
    payload = gram_of(payload, (0, 1, 2, 4, 5))
    receive(R1)
    receive_line(X0)
    first, second = apply_to(R1, X0)
    for b in range(own_rows):
        own[SENT + 1][b] = first[b]
        image[b] = jnp.where(flagged, vec_in[3, :, b, :] - second[b], 0.0)
    payload = gram_of(payload, (0, 1, 2, 4, 5, 6))
    receive(P2)
    for b, value in enumerate(apply_to(P2)[0]):
        own[SENT][b] = value
    payload = gram_of(payload, range(WIDTH))
    assert len(done) == len(MOMENTS)

    payload = jnp.sum(payload, axis=0, keepdims=True)
    gram_own[0] = payload
    gram_all[me] = payload

    def gram_copy(dd, rr):
        return pltpu.make_async_remote_copy(
            src_ref=gram_own.at[0],
            dst_ref=gram_all.at[me],
            send_sem=gram_send,
            recv_sem=gram_recv,
            device_id=(dd, rr),
            device_id_type=MESH,
        )

    @pl.loop(1, parts)
    def _(k):
        to = far_first(k)
        for rr in others + [r]:
            gram_copy(to, rr).start()

    for rr in others:
        gram_copy(d, rr).start()

    for v in range(SENT):
        sent(v)

    foreign = gram_all.at[pl.ds(0, parts * split - 1)]
    arrived(foreign, gram_send)
    arrived(foreign, gram_recv)

    whole = jnp.broadcast_to(jnp.sum(gram_all[...], axis=0), (cases, tb))
    entries = [
        jnp.broadcast_to(
            jnp.sum(jnp.where(entry_of == cases * e, whole, 0.0), axis=1, keepdims=True),
            (cases, tb),
        )
        for e in range(len(MOMENTS))
    ]
    gram = {pair: entries[ENTRY[moment_of(*pair)]] for pair in PAIRS}
    iterate_c, residual_c, direction_c = coefficients(gram)
    shifted_c = shifted_of(iterate_c)
    replace_c = {
        i: jnp.where(flagged, -shifted_c[i], w) if i in shifted_c else jnp.where(flagged, 0.0, w)
        for i, w in residual_c.items()
    }
    for b in range(own_rows):
        blocks = [ref[b] for ref in basis]

        def combine(total, weights_of):
            for i, w in weights_of.items():
                total = blocks[i] * w if total is None else total + blocks[i] * w
            return total

        out_ref[0, :, b, :] = combine(vec_in[2, :, b, :], iterate_c)
        out_ref[1, :, b, :] = combine(image[b], replace_c)
        out_ref[2, :, b, :] = combine(None, direction_c)


def write_out(made_ref, *refs):
    outs, sem = refs[:-1], refs[-1]
    copies = [
        pltpu.make_async_copy(made_ref.at[i], ref, sem.at[i]) for i, ref in enumerate(outs)
    ]
    for copy in copies:
        copy.start()
    for copy in copies:
        copy.wait()


def body(parts, split, tiles, rows, cols, sends, flags, right, iterate, residual, direction):
    cases, own_rows, tb = residual.shape
    gh = sends.shape[2]
    count = tiles.shape[0]
    f32 = jnp.float32
    dma = pltpu.SemaphoreType.DMA
    hbm = pl.BlockSpec(memory_space=pltpu.HBM)
    vmem = pl.BlockSpec(memory_space=pltpu.VMEM)
    scratch = (
        [pltpu.VMEM((split * own_rows + 2 * gh, cases, tb), f32)] * SENT
        + [pltpu.VMEM((own_rows, cases, tb), f32)] * (SENT + 3)
        + [pltpu.VMEM((2, gh, cases, tb), f32)] * SENT
        + [pltpu.VMEM((2, split, gh, cases, tb), f32)] * WIDE
        + [pltpu.VMEM((2, gh, cases, tb), f32)] * (SENT - WIDE)
        + [
            pltpu.VMEM((count, tb, tb), f32),
            pltpu.VMEM((count // 2, 2 * tb, 2 * tb), jnp.bfloat16),
            pltpu.VMEM((4, cases, own_rows, tb), f32),
            pltpu.VMEM((1, 1, tb), f32),
            pltpu.VMEM((parts * split, 1, tb), f32),
            pltpu.SMEM(rows.shape, jnp.int32),
            pltpu.SMEM(cols.shape, jnp.int32),
            pltpu.SMEM(sends.shape, jnp.int32),
            pltpu.SMEM(flags.shape, jnp.int32),
            dma((4,)),
            dma((4,)),
            dma((4,)),
            dma((SENT,)),
            dma((SENT,)),
            dma((SENT, 2)),
            dma((SENT, 2)),
            dma,
            dma,
        ]
    )
    made = pl.pallas_call(
        functools.partial(kernel, parts, split),
        out_shape=pltpu.VMEM((3, cases, own_rows, tb), f32),
        in_specs=[hbm] * 9,
        out_specs=vmem,
        scratch_shapes=scratch,
        compiler_params=pltpu.CompilerParams(
            collective_id=0, has_side_effects=True, vmem_limit_bytes=63 * 1024 * 1024
        ),
    )(rows, cols, sends, flags, tiles, direction, residual, iterate, right)
    return pl.pallas_call(
        write_out,
        out_shape=[jax.ShapeDtypeStruct(residual.shape, f32)] * 3,
        in_specs=[vmem],
        out_specs=[hbm] * 3,
        scratch_shapes=[dma((3,))],
    )(pltpu.with_memory_space_constraint(made, pltpu.VMEM))


def solution(mesh):
    both = ("dom", "rhs")
    vec = P(None, both, None)
    placed = (P(both, None, None), P(both), P(both), P("dom", None, None), P(), vec, vec, vec, vec)
    return jax.shard_map(
        functools.partial(body, mesh.shape["dom"], mesh.shape["rhs"]),
        mesh=mesh,
        in_specs=placed,
        out_specs=(vec, vec, vec),
        check_vma=False,
    )
```

```python
import functools

import jax
import jax.numpy as jnp
from jax import lax
from jax.experimental import pallas as pl
from jax.experimental.pallas import tpu as pltpu
from jax.sharding import PartitionSpec as P

SSTEP = 3
WIDTH = 2 * SSTEP + 1
P0, P1, P2, R1, R0, X0 = range(6)
WIDE = 4
SENT = 6
MESH = pl.DeviceIdType.MESH
UNROLL = 32


def moment_of(i, j):
    sides = (i > SSTEP) + (j > SSTEP)
    return sides, i + j - sides * (SSTEP + 1)


PAIRS = [(i, j) for i in range(WIDTH) for j in range(i, WIDTH)]
MOMENTS = sorted({moment_of(i, j) for i, j in PAIRS})
ENTRY = {moment: e for e, moment in enumerate(MOMENTS)}


def shifted_of(vec):
    return {i + 1: v for i, v in vec.items() if i not in (SSTEP, WIDTH - 1)}


def axpy(base, scale, other, sign):
    out = dict(base)
    for i, v in other.items():
        term = scale * v
        if i in out:
            out[i] = out[i] + term if sign > 0 else out[i] - term
        else:
            out[i] = term if sign > 0 else -term
    return out


def coefficients(gram):
    def quadratic(first, second):
        total = None
        for i, a in first.items():
            inner = None
            for j, b in second.items():
                term = gram[(min(i, j), max(i, j))] * b
                inner = term if inner is None else inner + term
            inner = inner * a
            total = inner if total is None else total + inner
        return total

    one = jnp.ones_like(gram[(0, 0)])
    direction = {0: one}
    residual = {SSTEP + 1: one}
    iterate = {}
    norm = quadratic(residual, residual)
    for _ in range(SSTEP):
        mapped = shifted_of(direction)
        step = norm / quadratic(direction, mapped)
        iterate = axpy(iterate, step, direction, 1)
        residual = axpy(residual, step, mapped, -1)
        next_norm = quadratic(residual, residual)
        direction = axpy(residual, next_norm / norm, direction, 1)
        norm = next_norm
    return iterate, residual, direction


def kernel(
    parts,
    split,
    rows_h,
    cols_h,
    sends_h,
    flags_h,
    tiles_h,
    direction_h,
    residual_h,
    iterate_h,
    right_h,
    out_ref,
    *scratch,
):
    scratch = list(scratch)
    take = lambda n: [scratch.pop(0) for _ in range(n)]
    ext = take(SENT)
    own = take(SENT + 3)
    ghost_send = take(SENT)
    ghost_recv = take(WIDE)
    line_recv = take(SENT - WIDE)
    tiles, weights, vec_in, gram_own, gram_all = take(5)
    rows_s, cols_s, sends_s, flags_s = take(4)
    tile_sem, vec_sem, index_sem, peer_send, peer_recv, side_send, side_recv = take(7)
    gram_send, gram_recv = take(2)

    d, r = lax.axis_index("dom"), lax.axis_index("rhs")
    cases, own_rows, tb = own[0].shape[1], own[0].shape[0], own[0].shape[2]
    gh = ghost_send[0].shape[1]
    tile_count = tiles.shape[0]
    chunks = tile_sem.shape[0]
    per_chunk = tile_count // chunks
    base = r * own_rows
    me = d * split + r
    has_left, has_right = d > 0, d < parts - 1
    core_count = 2 if split % 2 == 0 else 1
    chips = split // core_count
    others = []
    for h in range(1, chips):
        for c in range(core_count):
            chip = lax.rem(r // core_count + h, chips)
            others.append(chip * core_count + lax.rem(r + c, core_count))
    others += [
        r // core_count * core_count + lax.rem(r + c, core_count)
        for c in range(1, core_count)
    ]

    def far_first(k):
        down = parts - k - (parts - k <= d).astype(jnp.int32)
        up = k - 1 + (k - 1 >= d).astype(jnp.int32)
        return jnp.where(2 * d < parts, down, up)

    barrier = pltpu.get_barrier_semaphore()

    def greet(dd, rr):
        pl.semaphore_signal(barrier, inc=1, device_id=(dd, rr), device_id_type=MESH)

    @pl.loop(1, parts)
    def _(k):
        to = far_first(k)
        for rr in others + [r]:
            greet(to, rr)

    for rr in others:
        greet(d, rr)

    vec_copies = [
        pltpu.make_async_copy(ref, vec_in.at[i], vec_sem.at[i])
        for i, ref in enumerate((direction_h, residual_h, iterate_h, right_h))
    ]
    index_copies = [
        pltpu.make_async_copy(ref, to, index_sem.at[i])
        for i, (ref, to) in enumerate(
            ((sends_h, sends_s), (cols_h, cols_s), (rows_h, rows_s), (flags_h, flags_s))
        )
    ]
    vec_copies[0].start()
    index_copies[0].start()
    vec_copies[1].start()
    vec_copies[2].start()
    tile_copies = []
    for i in range(chunks):
        part = pl.ds(i * per_chunk, per_chunk)
        copy = pltpu.make_async_copy(tiles_h.at[part], tiles.at[part], tile_sem.at[i])
        copy.start()
        tile_copies.append(copy)
    for copy in vec_copies[3:] + index_copies[1:]:
        copy.start()

    first_ghost = split * own_rows
    for v in range(SENT):
        ext[v][pl.ds(first_ghost, 2 * gh)] = jnp.zeros((2 * gh, cases, tb), jnp.float32)

    def peer_copy(v, to):
        return pltpu.make_async_remote_copy(
            src_ref=own[v],
            dst_ref=ext[v].at[pl.ds(base, own_rows)],
            send_sem=peer_send.at[v],
            recv_sem=peer_recv.at[v],
            device_id=(d, to),
            device_id_type=MESH,
        )

    def side_copy(v, side, to):
        return pltpu.make_async_remote_copy(
            src_ref=ghost_send[v].at[side],
            dst_ref=ghost_recv[v].at[1 - side, r],
            send_sem=side_send.at[v, side],
            recv_sem=side_recv.at[v, 1 - side],
            device_id=(d - 1 + 2 * side, to),
            device_id_type=MESH,
        )

    def arrived(ref, sem):
        pltpu.make_async_copy(ref, ref, sem).wait()

    def keep(v, values):
        for b in range(own_rows):
            own[v][b] = values[b]
            ext[v][base + b] = values[b]

    def stage(v, values):
        keep(v, values)
        for side in range(2):
            for k in range(gh):
                local = sends_s[0, side, k] - base
                value = own[v][jnp.clip(local, 0, own_rows - 1)]
                where = jnp.full((cases, tb), local, jnp.int32)
                ghost_send[v][side, k] = jnp.where(
                    (where >= 0) & (where < own_rows), value, 0.0
                )

    early_side = lax.rem(d, 2)

    def send(v):
        for side in (early_side, 1 - early_side):

            @pl.when(jnp.where(side == 0, has_left, has_right))
            def _():
                for to in others + [r]:
                    side_copy(v, side, to).start()

        send_peers(v)

    def send_peers(v):
        for to in others:
            peer_copy(v, to).start()

    def receive_peers(v):
        arrived(ext[v].at[pl.ds(0, (split - 1) * own_rows)], peer_recv.at[v])

    def line_copy(v, side):
        return pltpu.make_async_remote_copy(
            src_ref=ghost_send[v].at[side],
            dst_ref=line_recv[v - WIDE].at[1 - side],
            send_sem=side_send.at[v, side],
            recv_sem=side_recv.at[v, 1 - side],
            device_id=(d - 1 + 2 * side, r),
            device_id_type=MESH,
        )

    def send_line(v):
        for side in range(2):
            for k in range(gh):
                ghost_send[v][side, k] = ext[v][sends_s[0, side, k]]
        for side, present in ((0, has_left), (1, has_right)):

            @pl.when(present)
            def _():
                line_copy(v, side).start()

    def receive_line(v):
        for side, present in ((0, has_left), (1, has_right)):

            @pl.when(present)
            def _():
                arrived(line_recv[v - WIDE].at[side], side_recv.at[v, side])
                ext[v][pl.ds(first_ghost + side * gh, gh)] = line_recv[v - WIDE][side]

    def receive(v):
        receive_peers(v)
        for side, present in ((0, has_left), (1, has_right)):

            @pl.when(present)
            def _():
                arrived(ghost_recv[v].at[side], side_recv.at[v, side])
                total = ghost_recv[v][side, 0]
                for o in range(1, split):
                    total = total + ghost_recv[v][side, o]
                ext[v][pl.ds(first_ghost + side * gh, gh)] = total

    def sent(v):
        arrived(ext[v].at[pl.ds(0, (split - 1) * own_rows)], peer_send.at[v])
        for side, present in ((0, has_left), (1, has_right)):

            @pl.when(present)
            def _():
                arrived(
                    ghost_recv[v].at[side] if v < WIDE else ghost_send[v].at[side],
                    side_send.at[v, side],
                )

    def input_blocks(i):
        return [vec_in[i, :, b, :] for b in range(own_rows)]

    low = lax.broadcasted_iota(jnp.int32, (2 * cases, tb), 0) < cases

    def apply_to(*vs):
        def step(i, accs):
            accs = list(accs)
            for u in range(UNROLL):
                q = i * UNROLL + u
                lhs = []
                for v in vs:
                    pair = jnp.concatenate(
                        [ext[v][cols_s[2 * q]], ext[v][cols_s[2 * q + 1]]], axis=0
                    )
                    high = pair.astype(jnp.bfloat16).astype(jnp.float32)
                    lhs += [high, pair - high]
                lhs = jnp.concatenate(lhs, axis=0).astype(jnp.bfloat16)
                lhs = jnp.concatenate([lhs, lhs], axis=1)
                out = jnp.dot(lhs, weights[q], preferred_element_type=jnp.float32)
                row = jnp.where(low, rows_s[2 * q], rows_s[2 * q + 1]) - base
                for n in range(len(vs)):
                    part = out[4 * cases * n : 4 * cases * (n + 1)]
                    part = part[: 2 * cases] + part[2 * cases :]
                    part = jnp.where(low, part[:, :tb], part[:, tb:])
                    for b in range(own_rows):
                        k = n * own_rows + b
                        accs[k] = accs[k] + jnp.where(row == b, part, 0.0)
            return tuple(accs)

        zero = jnp.zeros((2 * cases, tb), jnp.float32)
        accs = (zero,) * (own_rows * len(vs))
        accs = lax.fori_loop(0, tile_count // 2 // UNROLL, step, accs)
        sums = [a[:cases] + a[cases:] for a in accs]
        return [sums[n * own_rows : (n + 1) * own_rows] for n in range(len(vs))]

    index_copies[0].wait()
    vec_copies[0].wait()
    stage(P0, input_blocks(0))
    for i, v in ((1, R0), (2, X0)):
        vec_copies[i].wait()
        keep(v, input_blocks(i))
    pl.semaphore_wait(barrier, parts * split - 1)
    send(P0)
    send_peers(R0)
    for copy in vec_copies[3:] + index_copies[1:]:
        copy.wait()

    for i in range(chunks):
        tile_copies[i].wait()

        @pl.loop(i * per_chunk // 2, (i + 1) * per_chunk // 2)
        def _(q):
            for h in range(2):
                flipped = tiles[2 * q + h].T
                high = flipped.astype(jnp.bfloat16)
                weights[q, :tb, h * tb : (h + 1) * tb] = high
                weights[q, tb:, h * tb : (h + 1) * tb] = (
                    flipped - high.astype(jnp.float32)
                ).astype(jnp.bfloat16)

    case_of = lax.broadcasted_iota(jnp.int32, (cases, tb), 0)
    entry_of = lax.broadcasted_iota(jnp.int32, (cases, tb), 1) - case_of
    basis = [own[P0], own[P1], own[P2], own[SENT], own[R0], own[R1], own[SENT + 1]]
    image = own[SENT + 2]
    done = set()

    def gram_of(payload, known):
        for i, j in PAIRS:
            moment = moment_of(i, j)
            if moment in done or i not in known or j not in known:
                continue
            if abs(i - j) > 1 and moment[0] != 1:
                continue
            done.add(moment)
            total = basis[i][0] * basis[j][0]
            for b in range(1, own_rows):
                total = total + basis[i][b] * basis[j][b]
            total = jnp.sum(total, axis=1, keepdims=True)
            payload = payload + jnp.where(entry_of == cases * ENTRY[moment], total, 0.0)
        return payload

    receive_peers(R0)
    send_line(R0)
    receive(P0)
    stage(P1, apply_to(P0)[0])
    send(P1)
    send_peers(X0)
    flag = jnp.zeros((cases, tb), jnp.int32)
    for c in range(cases):
        flag = jnp.where(case_of == c, flags_s[c], flag)
    flagged = flag > 0
    receive_line(R0)
    stage(R1, apply_to(R0)[0])
    send(R1)
    payload = jnp.zeros((cases, tb), jnp.float32)
    payload = gram_of(payload, (0, 1, 4, 5))
    receive_peers(X0)
    send_line(X0)
    receive(P1)
    stage(P2, apply_to(P1)[0])
    send(P2)
    payload = gram_of(payload, (0, 1, 2, 4, 5))
    receive(R1)
    receive_line(X0)
    first, second = apply_to(R1, X0)
    for b in range(own_rows):
        own[SENT + 1][b] = first[b]
        image[b] = jnp.where(flagged, vec_in[3, :, b, :] - second[b], 0.0)
    payload = gram_of(payload, (0, 1, 2, 4, 5, 6))
    receive(P2)
    for b, value in enumerate(apply_to(P2)[0]):
        own[SENT][b] = value
    payload = gram_of(payload, range(WIDTH))
    assert len(done) == len(MOMENTS)

    payload = jnp.sum(payload, axis=0, keepdims=True)
    gram_own[0] = payload
    gram_all[me] = payload

    def gram_copy(dd, rr):
        return pltpu.make_async_remote_copy(
            src_ref=gram_own.at[0],
            dst_ref=gram_all.at[me],
            send_sem=gram_send,
            recv_sem=gram_recv,
            device_id=(dd, rr),
            device_id_type=MESH,
        )

    @pl.loop(1, parts)
    def _(k):
        to = far_first(k)
        for rr in others + [r]:
            gram_copy(to, rr).start()

    for rr in others:
        gram_copy(d, rr).start()

    for v in range(SENT):
        sent(v)

    foreign = gram_all.at[pl.ds(0, parts * split - 1)]
    arrived(foreign, gram_send)
    arrived(foreign, gram_recv)

    whole = jnp.broadcast_to(jnp.sum(gram_all[...], axis=0), (cases, tb))
    entries = [
        jnp.broadcast_to(
            jnp.sum(jnp.where(entry_of == cases * e, whole, 0.0), axis=1, keepdims=True),
            (cases, tb),
        )
        for e in range(len(MOMENTS))
    ]
    gram = {pair: entries[ENTRY[moment_of(*pair)]] for pair in PAIRS}
    iterate_c, residual_c, direction_c = coefficients(gram)
    shifted_c = shifted_of(iterate_c)
    replace_c = {
        i: jnp.where(flagged, -shifted_c[i], w) if i in shifted_c else jnp.where(flagged, 0.0, w)
        for i, w in residual_c.items()
    }
    for b in range(own_rows):
        blocks = [ref[b] for ref in basis]

        def combine(total, weights_of):
            for i, w in weights_of.items():
                total = blocks[i] * w if total is None else total + blocks[i] * w
            return total

        out_ref[0, :, b, :] = combine(vec_in[2, :, b, :], iterate_c)
        out_ref[1, :, b, :] = combine(image[b], replace_c)
        out_ref[2, :, b, :] = combine(None, direction_c)


def write_out(made_ref, *refs):
    outs, sem = refs[:-1], refs[-1]
    copies = [
        pltpu.make_async_copy(made_ref.at[i], ref, sem.at[i]) for i, ref in enumerate(outs)
    ]
    for copy in copies:
        copy.start()
    for copy in copies:
        copy.wait()


def body(parts, split, tiles, rows, cols, sends, flags, right, iterate, residual, direction):
    cases, own_rows, tb = residual.shape
    gh = sends.shape[2]
    count = tiles.shape[0]
    f32 = jnp.float32
    dma = pltpu.SemaphoreType.DMA
    hbm = pl.BlockSpec(memory_space=pltpu.HBM)
    vmem = pl.BlockSpec(memory_space=pltpu.VMEM)
    scratch = (
        [pltpu.VMEM((split * own_rows + 2 * gh, cases, tb), f32)] * SENT
        + [pltpu.VMEM((own_rows, cases, tb), f32)] * (SENT + 3)
        + [pltpu.VMEM((2, gh, cases, tb), f32)] * SENT
        + [pltpu.VMEM((2, split, gh, cases, tb), f32)] * WIDE
        + [pltpu.VMEM((2, gh, cases, tb), f32)] * (SENT - WIDE)
        + [
            pltpu.VMEM((count, tb, tb), f32),
            pltpu.VMEM((count // 2, 2 * tb, 2 * tb), jnp.bfloat16),
            pltpu.VMEM((4, cases, own_rows, tb), f32),
            pltpu.VMEM((1, 1, tb), f32),
            pltpu.VMEM((parts * split, 1, tb), f32),
            pltpu.SMEM(rows.shape, jnp.int32),
            pltpu.SMEM(cols.shape, jnp.int32),
            pltpu.SMEM(sends.shape, jnp.int32),
            pltpu.SMEM(flags.shape, jnp.int32),
            dma((4,)),
            dma((4,)),
            dma((4,)),
            dma((SENT,)),
            dma((SENT,)),
            dma((SENT, 2)),
            dma((SENT, 2)),
            dma,
            dma,
        ]
    )
    made = pl.pallas_call(
        functools.partial(kernel, parts, split),
        out_shape=pltpu.VMEM((3, cases, own_rows, tb), f32),
        in_specs=[hbm] * 9,
        out_specs=vmem,
        scratch_shapes=scratch,
        compiler_params=pltpu.CompilerParams(
            collective_id=0, has_side_effects=True, vmem_limit_bytes=63 * 1024 * 1024
        ),
    )(rows, cols, sends, flags, tiles, direction, residual, iterate, right)
    return pl.pallas_call(
        write_out,
        out_shape=[jax.ShapeDtypeStruct(residual.shape, f32)] * 3,
        in_specs=[vmem],
        out_specs=[hbm] * 3,
        scratch_shapes=[dma((3,))],
    )(pltpu.with_memory_space_constraint(made, pltpu.VMEM))


def solution(mesh):
    both = ("dom", "rhs")
    vec = P(None, both, None)
    placed = (P(both, None, None), P(both), P(both), P("dom", None, None), P(), vec, vec, vec, vec)
    return jax.shard_map(
        functools.partial(body, mesh.shape["dom"], mesh.shape["rhs"]),
        mesh=mesh,
        in_specs=placed,
        out_specs=(vec, vec, vec),
        check_vma=False,
    )
```

```python
import functools

import jax
import jax.numpy as jnp
from jax import lax
from jax.experimental import pallas as pl
from jax.experimental.pallas import tpu as pltpu
from jax.sharding import PartitionSpec as P

SSTEP = 3
WIDTH = 2 * SSTEP + 1
P0, P1, P2, R1, R0, X0 = range(6)
WIDE = 4
SENT = 6
MESH = pl.DeviceIdType.MESH
UNROLL = 32


def moment_of(i, j):
    sides = (i > SSTEP) + (j > SSTEP)
    return sides, i + j - sides * (SSTEP + 1)


PAIRS = [(i, j) for i in range(WIDTH) for j in range(i, WIDTH)]
MOMENTS = sorted({moment_of(i, j) for i, j in PAIRS})
ENTRY = {moment: e for e, moment in enumerate(MOMENTS)}


def shifted_of(vec):
    return {i + 1: v for i, v in vec.items() if i not in (SSTEP, WIDTH - 1)}


def axpy(base, scale, other, sign):
    out = dict(base)
    for i, v in other.items():
        term = scale * v
        if i in out:
            out[i] = out[i] + term if sign > 0 else out[i] - term
        else:
            out[i] = term if sign > 0 else -term
    return out


def coefficients(gram):
    def quadratic(first, second):
        total = None
        for i, a in first.items():
            inner = None
            for j, b in second.items():
                term = gram[(min(i, j), max(i, j))] * b
                inner = term if inner is None else inner + term
            inner = inner * a
            total = inner if total is None else total + inner
        return total

    one = jnp.ones_like(gram[(0, 0)])
    direction = {0: one}
    residual = {SSTEP + 1: one}
    iterate = {}
    norm = quadratic(residual, residual)
    for _ in range(SSTEP):
        mapped = shifted_of(direction)
        step = norm / quadratic(direction, mapped)
        iterate = axpy(iterate, step, direction, 1)
        residual = axpy(residual, step, mapped, -1)
        next_norm = quadratic(residual, residual)
        direction = axpy(residual, next_norm / norm, direction, 1)
        norm = next_norm
    return iterate, residual, direction


def kernel(
    parts,
    split,
    rows_h,
    cols_h,
    sends_h,
    flags_h,
    tiles_h,
    direction_h,
    residual_h,
    iterate_h,
    right_h,
    out_ref,
    *scratch,
):
    scratch = list(scratch)
    take = lambda n: [scratch.pop(0) for _ in range(n)]
    ext = take(SENT)
    own = take(SENT + 3)
    ghost_send = take(SENT)
    ghost_recv = take(WIDE)
    line_recv = take(SENT - WIDE)
    tiles, weights, vec_in, gram_own, gram_all = take(5)
    rows_s, cols_s, sends_s, flags_s = take(4)
    tile_sem, vec_sem, index_sem, peer_send, peer_recv, side_send, side_recv = take(7)
    gram_send, gram_recv, known = take(3)

    d, r = lax.axis_index("dom"), lax.axis_index("rhs")
    cases, own_rows, tb = own[0].shape[1], own[0].shape[0], own[0].shape[2]
    gh = ghost_send[0].shape[1]
    tile_count = tiles.shape[0]
    chunks = tile_sem.shape[0]
    per_chunk = tile_count // chunks
    base = r * own_rows
    me = d * split + r
    has_left, has_right = d > 0, d < parts - 1
    core_count = 2 if split % 2 == 0 else 1
    chips = split // core_count
    others = []
    for h in range(1, chips):
        for c in range(core_count):
            chip = lax.rem(r // core_count + h, chips)
            others.append(chip * core_count + lax.rem(r + c, core_count))
    others += [
        r // core_count * core_count + lax.rem(r + c, core_count)
        for c in range(1, core_count)
    ]

    def far_first(k):
        down = parts - k - (parts - k <= d).astype(jnp.int32)
        up = k - 1 + (k - 1 >= d).astype(jnp.int32)
        return jnp.where(2 * d < parts, down, up)

    barrier = pltpu.get_barrier_semaphore()

    def greet(dd, rr):
        pl.semaphore_signal(barrier, inc=1, device_id=(dd, rr), device_id_type=MESH)

    for dd, present in ((d - 1, has_left), (d + 1, has_right)):

        @pl.when(present)
        def _():
            for rr in others + [r]:
                greet(dd, rr)

    for rr in others:
        greet(d, rr)

    reaches = []
    while (reaches[-1] * 2 if reaches else 1) < parts - 1:
        reaches.append(2 ** len(reaches))
    passed = []

    def spread(k):
        reach = reaches[k]
        for dd, present in ((d - reach, d >= reach), (d + reach, d + reach < parts)):

            @pl.when(present)
            def _():
                pl.semaphore_signal(
                    known.at[k], inc=1, device_id=(dd, r), device_id_type=MESH
                )

    def advance():
        k = len(passed)
        if k < len(reaches):
            reach = reaches[k]
            both = (d >= reach).astype(jnp.int32) + (d + reach < parts).astype(jnp.int32)
            pl.semaphore_wait(known.at[k], both)
            passed.append(k)
            if k + 1 < len(reaches):
                spread(k + 1)

    vec_copies = [
        pltpu.make_async_copy(ref, vec_in.at[i], vec_sem.at[i])
        for i, ref in enumerate((direction_h, residual_h, iterate_h, right_h))
    ]
    index_copies = [
        pltpu.make_async_copy(ref, to, index_sem.at[i])
        for i, (ref, to) in enumerate(
            ((sends_h, sends_s), (cols_h, cols_s), (rows_h, rows_s), (flags_h, flags_s))
        )
    ]
    vec_copies[0].start()
    index_copies[0].start()
    vec_copies[1].start()
    vec_copies[2].start()
    tile_copies = []
    for i in range(chunks):
        part = pl.ds(i * per_chunk, per_chunk)
        copy = pltpu.make_async_copy(tiles_h.at[part], tiles.at[part], tile_sem.at[i])
        copy.start()
        tile_copies.append(copy)
    for copy in vec_copies[3:] + index_copies[1:]:
        copy.start()

    first_ghost = split * own_rows
    for v in range(SENT):
        ext[v][pl.ds(first_ghost, 2 * gh)] = jnp.zeros((2 * gh, cases, tb), jnp.float32)

    def peer_copy(v, to):
        return pltpu.make_async_remote_copy(
            src_ref=own[v],
            dst_ref=ext[v].at[pl.ds(base, own_rows)],
            send_sem=peer_send.at[v],
            recv_sem=peer_recv.at[v],
            device_id=(d, to),
            device_id_type=MESH,
        )

    def side_copy(v, side, to):
        return pltpu.make_async_remote_copy(
            src_ref=ghost_send[v].at[side],
            dst_ref=ghost_recv[v].at[1 - side, r],
            send_sem=side_send.at[v, side],
            recv_sem=side_recv.at[v, 1 - side],
            device_id=(d - 1 + 2 * side, to),
            device_id_type=MESH,
        )

    def arrived(ref, sem):
        pltpu.make_async_copy(ref, ref, sem).wait()

    def keep(v, values):
        for b in range(own_rows):
            own[v][b] = values[b]
            ext[v][base + b] = values[b]

    def stage(v, values):
        keep(v, values)
        for side in range(2):
            for k in range(gh):
                local = sends_s[0, side, k] - base
                value = own[v][jnp.clip(local, 0, own_rows - 1)]
                where = jnp.full((cases, tb), local, jnp.int32)
                ghost_send[v][side, k] = jnp.where(
                    (where >= 0) & (where < own_rows), value, 0.0
                )

    early_side = lax.rem(d, 2)

    def send(v):
        for side in (early_side, 1 - early_side):

            @pl.when(jnp.where(side == 0, has_left, has_right))
            def _():
                for to in others + [r]:
                    side_copy(v, side, to).start()

        send_peers(v)

    def send_peers(v):
        for to in others:
            peer_copy(v, to).start()

    def receive_peers(v):
        arrived(ext[v].at[pl.ds(0, (split - 1) * own_rows)], peer_recv.at[v])

    def line_copy(v, side):
        return pltpu.make_async_remote_copy(
            src_ref=ghost_send[v].at[side],
            dst_ref=line_recv[v - WIDE].at[1 - side],
            send_sem=side_send.at[v, side],
            recv_sem=side_recv.at[v, 1 - side],
            device_id=(d - 1 + 2 * side, r),
            device_id_type=MESH,
        )

    def send_line(v):
        for side in range(2):
            for k in range(gh):
                ghost_send[v][side, k] = ext[v][sends_s[0, side, k]]
        for side, present in ((0, has_left), (1, has_right)):

            @pl.when(present)
            def _():
                line_copy(v, side).start()

    def receive_line(v):
        for side, present in ((0, has_left), (1, has_right)):

            @pl.when(present)
            def _():
                arrived(line_recv[v - WIDE].at[side], side_recv.at[v, side])
                ext[v][pl.ds(first_ghost + side * gh, gh)] = line_recv[v - WIDE][side]

    def receive(v):
        receive_peers(v)
        for side, present in ((0, has_left), (1, has_right)):

            @pl.when(present)
            def _():
                arrived(ghost_recv[v].at[side], side_recv.at[v, side])
                total = ghost_recv[v][side, 0]
                for o in range(1, split):
                    total = total + ghost_recv[v][side, o]
                ext[v][pl.ds(first_ghost + side * gh, gh)] = total

    def sent(v):
        arrived(ext[v].at[pl.ds(0, (split - 1) * own_rows)], peer_send.at[v])
        for side, present in ((0, has_left), (1, has_right)):

            @pl.when(present)
            def _():
                arrived(
                    ghost_recv[v].at[side] if v < WIDE else ghost_send[v].at[side],
                    side_send.at[v, side],
                )

    def input_blocks(i):
        return [vec_in[i, :, b, :] for b in range(own_rows)]

    low = lax.broadcasted_iota(jnp.int32, (2 * cases, tb), 0) < cases

    def apply_to(*vs):
        def step(i, accs):
            accs = list(accs)
            for u in range(UNROLL):
                q = i * UNROLL + u
                lhs = []
                for v in vs:
                    pair = jnp.concatenate(
                        [ext[v][cols_s[2 * q]], ext[v][cols_s[2 * q + 1]]], axis=0
                    )
                    high = pair.astype(jnp.bfloat16).astype(jnp.float32)
                    lhs += [high, pair - high]
                lhs = jnp.concatenate(lhs, axis=0).astype(jnp.bfloat16)
                lhs = jnp.concatenate([lhs, lhs], axis=1)
                out = jnp.dot(lhs, weights[q], preferred_element_type=jnp.float32)
                row = jnp.where(low, rows_s[2 * q], rows_s[2 * q + 1]) - base
                for n in range(len(vs)):
                    part = out[4 * cases * n : 4 * cases * (n + 1)]
                    part = part[: 2 * cases] + part[2 * cases :]
                    part = jnp.where(low, part[:, :tb], part[:, tb:])
                    for b in range(own_rows):
                        k = n * own_rows + b
                        accs[k] = accs[k] + jnp.where(row == b, part, 0.0)
            return tuple(accs)

        zero = jnp.zeros((2 * cases, tb), jnp.float32)
        accs = (zero,) * (own_rows * len(vs))
        accs = lax.fori_loop(0, tile_count // 2 // UNROLL, step, accs)
        sums = [a[:cases] + a[cases:] for a in accs]
        return [sums[n * own_rows : (n + 1) * own_rows] for n in range(len(vs))]

    index_copies[0].wait()
    vec_copies[0].wait()
    stage(P0, input_blocks(0))
    for i, v in ((1, R0), (2, X0)):
        vec_copies[i].wait()
        keep(v, input_blocks(i))
    sides = has_left.astype(jnp.int32) + has_right.astype(jnp.int32)
    pl.semaphore_wait(barrier, split - 1 + split * sides)
    send(P0)
    send_peers(R0)
    if reaches:
        spread(0)
    for copy in vec_copies[3:] + index_copies[1:]:
        copy.wait()

    for i in range(chunks):
        tile_copies[i].wait()

        @pl.loop(i * per_chunk // 2, (i + 1) * per_chunk // 2)
        def _(q):
            for h in range(2):
                flipped = tiles[2 * q + h].T
                high = flipped.astype(jnp.bfloat16)
                weights[q, :tb, h * tb : (h + 1) * tb] = high
                weights[q, tb:, h * tb : (h + 1) * tb] = (
                    flipped - high.astype(jnp.float32)
                ).astype(jnp.bfloat16)

    case_of = lax.broadcasted_iota(jnp.int32, (cases, tb), 0)
    entry_of = lax.broadcasted_iota(jnp.int32, (cases, tb), 1) - case_of
    basis = [own[P0], own[P1], own[P2], own[SENT], own[R0], own[R1], own[SENT + 1]]
    image = own[SENT + 2]
    done = set()

    def gram_of(payload, known):
        for i, j in PAIRS:
            moment = moment_of(i, j)
            if moment in done or i not in known or j not in known:
                continue
            if abs(i - j) > 1 and moment[0] != 1:
                continue
            done.add(moment)
            total = basis[i][0] * basis[j][0]
            for b in range(1, own_rows):
                total = total + basis[i][b] * basis[j][b]
            total = jnp.sum(total, axis=1, keepdims=True)
            payload = payload + jnp.where(entry_of == cases * ENTRY[moment], total, 0.0)
        return payload

    receive_peers(R0)
    send_line(R0)
    send_peers(X0)
    receive(P0)
    advance()
    stage(P1, apply_to(P0)[0])
    send(P1)
    flag = jnp.zeros((cases, tb), jnp.int32)
    for c in range(cases):
        flag = jnp.where(case_of == c, flags_s[c], flag)
    flagged = flag > 0
    receive_line(R0)
    stage(R1, apply_to(R0)[0])
    send(R1)
    payload = jnp.zeros((cases, tb), jnp.float32)
    payload = gram_of(payload, (0, 1, 4, 5))
    receive_peers(X0)
    send_line(X0)
    receive(P1)
    advance()
    stage(P2, apply_to(P1)[0])
    send(P2)
    payload = gram_of(payload, (0, 1, 2, 4, 5))
    receive(R1)
    receive_line(X0)
    first, second = apply_to(R1, X0)
    for b in range(own_rows):
        own[SENT + 1][b] = first[b]
        image[b] = jnp.where(flagged, vec_in[3, :, b, :] - second[b], 0.0)
    payload = gram_of(payload, (0, 1, 2, 4, 5, 6))
    while len(passed) < len(reaches):
        advance()
    receive(P2)
    for b, value in enumerate(apply_to(P2)[0]):
        own[SENT][b] = value
    payload = gram_of(payload, range(WIDTH))
    assert len(done) == len(MOMENTS)

    payload = jnp.sum(payload, axis=0, keepdims=True)
    gram_own[0] = payload
    gram_all[me] = payload

    def gram_copy(dd, rr):
        return pltpu.make_async_remote_copy(
            src_ref=gram_own.at[0],
            dst_ref=gram_all.at[me],
            send_sem=gram_send,
            recv_sem=gram_recv,
            device_id=(dd, rr),
            device_id_type=MESH,
        )

    @pl.loop(1, parts)
    def _(k):
        to = far_first(k)
        for rr in others + [r]:
            gram_copy(to, rr).start()

    for rr in others:
        gram_copy(d, rr).start()

    for v in range(SENT):
        sent(v)

    foreign = gram_all.at[pl.ds(0, parts * split - 1)]
    arrived(foreign, gram_send)
    arrived(foreign, gram_recv)

    whole = jnp.broadcast_to(jnp.sum(gram_all[...], axis=0), (cases, tb))
    entries = [
        jnp.broadcast_to(
            jnp.sum(jnp.where(entry_of == cases * e, whole, 0.0), axis=1, keepdims=True),
            (cases, tb),
        )
        for e in range(len(MOMENTS))
    ]
    gram = {pair: entries[ENTRY[moment_of(*pair)]] for pair in PAIRS}
    iterate_c, residual_c, direction_c = coefficients(gram)
    shifted_c = shifted_of(iterate_c)
    replace_c = {
        i: jnp.where(flagged, -shifted_c[i], w) if i in shifted_c else jnp.where(flagged, 0.0, w)
        for i, w in residual_c.items()
    }
    for b in range(own_rows):
        blocks = [ref[b] for ref in basis]

        def combine(total, weights_of):
            for i, w in weights_of.items():
                total = blocks[i] * w if total is None else total + blocks[i] * w
            return total

        out_ref[0, :, b, :] = combine(vec_in[2, :, b, :], iterate_c)
        out_ref[1, :, b, :] = combine(image[b], replace_c)
        out_ref[2, :, b, :] = combine(None, direction_c)


def write_out(made_ref, *refs):
    outs, sem = refs[:-1], refs[-1]
    copies = [
        pltpu.make_async_copy(made_ref.at[i], ref, sem.at[i]) for i, ref in enumerate(outs)
    ]
    for copy in copies:
        copy.start()
    for copy in copies:
        copy.wait()


def body(parts, split, tiles, rows, cols, sends, flags, right, iterate, residual, direction):
    cases, own_rows, tb = residual.shape
    gh = sends.shape[2]
    count = tiles.shape[0]
    f32 = jnp.float32
    dma = pltpu.SemaphoreType.DMA
    hbm = pl.BlockSpec(memory_space=pltpu.HBM)
    vmem = pl.BlockSpec(memory_space=pltpu.VMEM)
    scratch = (
        [pltpu.VMEM((split * own_rows + 2 * gh, cases, tb), f32)] * SENT
        + [pltpu.VMEM((own_rows, cases, tb), f32)] * (SENT + 3)
        + [pltpu.VMEM((2, gh, cases, tb), f32)] * SENT
        + [pltpu.VMEM((2, split, gh, cases, tb), f32)] * WIDE
        + [pltpu.VMEM((2, gh, cases, tb), f32)] * (SENT - WIDE)
        + [
            pltpu.VMEM((count, tb, tb), f32),
            pltpu.VMEM((count // 2, 2 * tb, 2 * tb), jnp.bfloat16),
            pltpu.VMEM((4, cases, own_rows, tb), f32),
            pltpu.VMEM((1, 1, tb), f32),
            pltpu.VMEM((parts * split, 1, tb), f32),
            pltpu.SMEM(rows.shape, jnp.int32),
            pltpu.SMEM(cols.shape, jnp.int32),
            pltpu.SMEM(sends.shape, jnp.int32),
            pltpu.SMEM(flags.shape, jnp.int32),
            dma((4,)),
            dma((4,)),
            dma((4,)),
            dma((SENT,)),
            dma((SENT,)),
            dma((SENT, 2)),
            dma((SENT, 2)),
            dma,
            dma,
            pltpu.SemaphoreType.REGULAR((max(parts.bit_length(), 1),)),
        ]
    )
    made = pl.pallas_call(
        functools.partial(kernel, parts, split),
        out_shape=pltpu.VMEM((3, cases, own_rows, tb), f32),
        in_specs=[hbm] * 9,
        out_specs=vmem,
        scratch_shapes=scratch,
        compiler_params=pltpu.CompilerParams(
            collective_id=0, has_side_effects=True, vmem_limit_bytes=63 * 1024 * 1024
        ),
    )(rows, cols, sends, flags, tiles, direction, residual, iterate, right)
    return pl.pallas_call(
        write_out,
        out_shape=[jax.ShapeDtypeStruct(residual.shape, f32)] * 3,
        in_specs=[vmem],
        out_specs=[hbm] * 3,
        scratch_shapes=[dma((3,))],
    )(pltpu.with_memory_space_constraint(made, pltpu.VMEM))


def solution(mesh):
    both = ("dom", "rhs")
    vec = P(None, both, None)
    placed = (P(both, None, None), P(both), P(both), P("dom", None, None), P(), vec, vec, vec, vec)
    return jax.shard_map(
        functools.partial(body, mesh.shape["dom"], mesh.shape["rhs"]),
        mesh=mesh,
        in_specs=placed,
        out_specs=(vec, vec, vec),
        check_vma=False,
    )
```

```python
import functools

import jax
import jax.numpy as jnp
from jax import lax
from jax.experimental import pallas as pl
from jax.experimental.pallas import tpu as pltpu
from jax.sharding import PartitionSpec as P

SSTEP = 3
WIDTH = 2 * SSTEP + 1
P0, P1, P2, R1, R0, X0 = range(6)
WIDE = 4
SENT = 6
MESH = pl.DeviceIdType.MESH
UNROLL = 32


def moment_of(i, j):
    sides = (i > SSTEP) + (j > SSTEP)
    return sides, i + j - sides * (SSTEP + 1)


PAIRS = [(i, j) for i in range(WIDTH) for j in range(i, WIDTH)]
MOMENTS = sorted({moment_of(i, j) for i, j in PAIRS})
ENTRY = {moment: e for e, moment in enumerate(MOMENTS)}


def shifted_of(vec):
    return {i + 1: v for i, v in vec.items() if i not in (SSTEP, WIDTH - 1)}


def axpy(base, scale, other, sign):
    out = dict(base)
    for i, v in other.items():
        term = scale * v
        if i in out:
            out[i] = out[i] + term if sign > 0 else out[i] - term
        else:
            out[i] = term if sign > 0 else -term
    return out


def coefficients(gram):
    def quadratic(first, second):
        total = None
        for i, a in first.items():
            inner = None
            for j, b in second.items():
                term = gram[(min(i, j), max(i, j))] * b
                inner = term if inner is None else inner + term
            inner = inner * a
            total = inner if total is None else total + inner
        return total

    one = jnp.ones_like(gram[(0, 0)])
    direction = {0: one}
    residual = {SSTEP + 1: one}
    iterate = {}
    norm = quadratic(residual, residual)
    for _ in range(SSTEP):
        mapped = shifted_of(direction)
        step = norm / quadratic(direction, mapped)
        iterate = axpy(iterate, step, direction, 1)
        residual = axpy(residual, step, mapped, -1)
        next_norm = quadratic(residual, residual)
        direction = axpy(residual, next_norm / norm, direction, 1)
        norm = next_norm
    return iterate, residual, direction


def kernel(
    parts,
    split,
    rows_h,
    cols_h,
    sends_h,
    flags_h,
    tiles_h,
    direction_h,
    residual_h,
    iterate_h,
    right_h,
    out_ref,
    *scratch,
):
    scratch = list(scratch)
    take = lambda n: [scratch.pop(0) for _ in range(n)]
    ext = take(SENT)
    own = take(SENT + 3)
    ghost_send = take(SENT)
    ghost_recv = take(WIDE)
    line_recv = take(SENT - WIDE)
    tiles, weights, vec_in, gram_own, gram_all = take(5)
    rows_s, cols_s, sends_s, flags_s = take(4)
    tile_sem, vec_sem, index_sem, peer_send, peer_recv, side_send, side_recv = take(7)
    gram_send, gram_recv, known = take(3)

    d, r = lax.axis_index("dom"), lax.axis_index("rhs")
    cases, own_rows, tb = own[0].shape[1], own[0].shape[0], own[0].shape[2]
    gh = ghost_send[0].shape[1]
    tile_count = tiles.shape[0]
    chunks = tile_sem.shape[0]
    per_chunk = tile_count // chunks
    base = r * own_rows
    me = d * split + r
    has_left, has_right = d > 0, d < parts - 1
    core_count = 2 if split % 2 == 0 else 1
    chips = split // core_count
    others = []
    for h in range(1, chips):
        for c in range(core_count):
            chip = lax.rem(r // core_count + h, chips)
            others.append(chip * core_count + lax.rem(r + c, core_count))
    others += [
        r // core_count * core_count + lax.rem(r + c, core_count)
        for c in range(1, core_count)
    ]

    def far_first(k):
        down = parts - k - (parts - k <= d).astype(jnp.int32)
        up = k - 1 + (k - 1 >= d).astype(jnp.int32)
        return jnp.where(2 * d < parts, down, up)

    barrier = pltpu.get_barrier_semaphore()

    def greet(dd, rr):
        pl.semaphore_signal(barrier, inc=1, device_id=(dd, rr), device_id_type=MESH)

    for dd, present in ((d - 1, has_left), (d + 1, has_right)):

        @pl.when(present)
        def _():
            for rr in others + [r]:
                greet(dd, rr)

    for rr in others:
        greet(d, rr)

    reaches = []
    while (reaches[-1] * 2 if reaches else 1) < parts - 1:
        reaches.append(2 ** len(reaches))
    passed = []

    def spread(k):
        reach = reaches[k]
        for dd, present in ((d - reach, d >= reach), (d + reach, d + reach < parts)):

            @pl.when(present)
            def _():
                pl.semaphore_signal(
                    known.at[k], inc=1, device_id=(dd, r), device_id_type=MESH
                )

    def advance():
        k = len(passed)
        if k < len(reaches):
            reach = reaches[k]
            both = (d >= reach).astype(jnp.int32) + (d + reach < parts).astype(jnp.int32)
            pl.semaphore_wait(known.at[k], both)
            passed.append(k)
            if k + 1 < len(reaches):
                spread(k + 1)

    vec_copies = [
        pltpu.make_async_copy(ref, vec_in.at[i], vec_sem.at[i])
        for i, ref in enumerate((direction_h, residual_h, iterate_h, right_h))
    ]
    index_copies = [
        pltpu.make_async_copy(ref, to, index_sem.at[i])
        for i, (ref, to) in enumerate(
            ((sends_h, sends_s), (cols_h, cols_s), (rows_h, rows_s), (flags_h, flags_s))
        )
    ]
    vec_copies[0].start()
    index_copies[0].start()
    vec_copies[1].start()
    vec_copies[2].start()
    tile_copies = []
    for i in range(chunks):
        part = pl.ds(i * per_chunk, per_chunk)
        copy = pltpu.make_async_copy(tiles_h.at[part], tiles.at[part], tile_sem.at[i])
        copy.start()
        tile_copies.append(copy)
    for copy in vec_copies[3:] + index_copies[1:]:
        copy.start()

    first_ghost = split * own_rows
    for v in range(SENT):
        ext[v][pl.ds(first_ghost, 2 * gh)] = jnp.zeros((2 * gh, cases, tb), jnp.float32)

    def peer_copy(v, to):
        return pltpu.make_async_remote_copy(
            src_ref=own[v],
            dst_ref=ext[v].at[pl.ds(base, own_rows)],
            send_sem=peer_send.at[v],
            recv_sem=peer_recv.at[v],
            device_id=(d, to),
            device_id_type=MESH,
        )

    def side_copy(v, side, to):
        return pltpu.make_async_remote_copy(
            src_ref=ghost_send[v].at[side],
            dst_ref=ghost_recv[v].at[1 - side, r],
            send_sem=side_send.at[v, side],
            recv_sem=side_recv.at[v, 1 - side],
            device_id=(d - 1 + 2 * side, to),
            device_id_type=MESH,
        )

    def arrived(ref, sem):
        pltpu.make_async_copy(ref, ref, sem).wait()

    def keep(v, values):
        for b in range(own_rows):
            own[v][b] = values[b]
            ext[v][base + b] = values[b]

    def stage(v, values):
        keep(v, values)
        for side in range(2):
            for k in range(gh):
                local = sends_s[0, side, k] - base
                value = own[v][jnp.clip(local, 0, own_rows - 1)]
                where = jnp.full((cases, tb), local, jnp.int32)
                ghost_send[v][side, k] = jnp.where(
                    (where >= 0) & (where < own_rows), value, 0.0
                )

    early_side = lax.rem(d, 2)

    def send(v):
        for side in (early_side, 1 - early_side):

            @pl.when(jnp.where(side == 0, has_left, has_right))
            def _():
                for to in others + [r]:
                    side_copy(v, side, to).start()

        send_peers(v)

    def send_peers(v):
        for to in others:
            peer_copy(v, to).start()

    def receive_peers(v):
        arrived(ext[v].at[pl.ds(0, (split - 1) * own_rows)], peer_recv.at[v])

    def line_copy(v, side):
        return pltpu.make_async_remote_copy(
            src_ref=ghost_send[v].at[side],
            dst_ref=line_recv[v - WIDE].at[1 - side],
            send_sem=side_send.at[v, side],
            recv_sem=side_recv.at[v, 1 - side],
            device_id=(d - 1 + 2 * side, r),
            device_id_type=MESH,
        )

    def send_line(v):
        for side in range(2):
            for k in range(gh):
                ghost_send[v][side, k] = ext[v][sends_s[0, side, k]]
        for side, present in ((0, has_left), (1, has_right)):

            @pl.when(present)
            def _():
                line_copy(v, side).start()

    def receive_line(v):
        for side, present in ((0, has_left), (1, has_right)):

            @pl.when(present)
            def _():
                arrived(line_recv[v - WIDE].at[side], side_recv.at[v, side])
                ext[v][pl.ds(first_ghost + side * gh, gh)] = line_recv[v - WIDE][side]

    def receive(v):
        receive_peers(v)
        for side, present in ((0, has_left), (1, has_right)):

            @pl.when(present)
            def _():
                arrived(ghost_recv[v].at[side], side_recv.at[v, side])
                total = ghost_recv[v][side, 0]
                for o in range(1, split):
                    total = total + ghost_recv[v][side, o]
                ext[v][pl.ds(first_ghost + side * gh, gh)] = total

    def sent(v):
        arrived(ext[v].at[pl.ds(0, (split - 1) * own_rows)], peer_send.at[v])
        for side, present in ((0, has_left), (1, has_right)):

            @pl.when(present)
            def _():
                arrived(
                    ghost_recv[v].at[side] if v < WIDE else ghost_send[v].at[side],
                    side_send.at[v, side],
                )

    def input_blocks(i):
        return [vec_in[i, :, b, :] for b in range(own_rows)]

    low = lax.broadcasted_iota(jnp.int32, (2 * cases, tb), 0) < cases

    def apply_to(*vs):
        def step(i, accs):
            accs = list(accs)
            for u in range(UNROLL):
                q = i * UNROLL + u
                lhs = []
                for v in vs:
                    pair = jnp.concatenate(
                        [ext[v][cols_s[2 * q]], ext[v][cols_s[2 * q + 1]]], axis=0
                    )
                    high = pair.astype(jnp.bfloat16).astype(jnp.float32)
                    lhs += [high, pair - high]
                lhs = jnp.concatenate(lhs, axis=0).astype(jnp.bfloat16)
                lhs = jnp.concatenate([lhs, lhs], axis=1)
                out = jnp.dot(lhs, weights[q], preferred_element_type=jnp.float32)
                row = jnp.where(low, rows_s[2 * q], rows_s[2 * q + 1]) - base
                for n in range(len(vs)):
                    part = out[4 * cases * n : 4 * cases * (n + 1)]
                    part = part[: 2 * cases] + part[2 * cases :]
                    part = jnp.where(low, part[:, :tb], part[:, tb:])
                    for b in range(own_rows):
                        k = n * own_rows + b
                        accs[k] = accs[k] + jnp.where(row == b, part, 0.0)
            return tuple(accs)

        zero = jnp.zeros((2 * cases, tb), jnp.float32)
        accs = (zero,) * (own_rows * len(vs))
        accs = lax.fori_loop(0, tile_count // 2 // UNROLL, step, accs)
        sums = [a[:cases] + a[cases:] for a in accs]
        return [sums[n * own_rows : (n + 1) * own_rows] for n in range(len(vs))]

    index_copies[0].wait()
    vec_copies[0].wait()
    stage(P0, input_blocks(0))
    vec_copies[1].wait()
    keep(R0, input_blocks(1))
    sides = has_left.astype(jnp.int32) + has_right.astype(jnp.int32)
    pl.semaphore_wait(barrier, split - 1 + split * sides)
    send(P0)
    send_peers(R0)
    if reaches:
        spread(0)
    for copy in vec_copies[2:] + index_copies[1:]:
        copy.wait()

    for i in range(chunks):
        tile_copies[i].wait()

        @pl.loop(i * per_chunk // 2, (i + 1) * per_chunk // 2)
        def _(q):
            for h in range(2):
                flipped = tiles[2 * q + h].T
                high = flipped.astype(jnp.bfloat16)
                weights[q, :tb, h * tb : (h + 1) * tb] = high
                weights[q, tb:, h * tb : (h + 1) * tb] = (
                    flipped - high.astype(jnp.float32)
                ).astype(jnp.bfloat16)

    case_of = lax.broadcasted_iota(jnp.int32, (cases, tb), 0)
    entry_of = lax.broadcasted_iota(jnp.int32, (cases, tb), 1) - case_of
    basis = [own[P0], own[P1], own[P2], own[SENT], own[R0], own[R1], own[SENT + 1]]
    image = own[SENT + 2]
    done = set()

    def gram_of(payload, known):
        for i, j in PAIRS:
            moment = moment_of(i, j)
            if moment in done or i not in known or j not in known:
                continue
            if abs(i - j) > 1 and moment[0] != 1:
                continue
            done.add(moment)
            total = basis[i][0] * basis[j][0]
            for b in range(1, own_rows):
                total = total + basis[i][b] * basis[j][b]
            total = jnp.sum(total, axis=1, keepdims=True)
            payload = payload + jnp.where(entry_of == cases * ENTRY[moment], total, 0.0)
        return payload

    receive_peers(R0)
    send_line(R0)
    receive(P0)
    advance()
    stage(P1, apply_to(P0)[0])
    send(P1)
    flag = jnp.zeros((cases, tb), jnp.int32)
    for c in range(cases):
        flag = jnp.where(case_of == c, flags_s[c], flag)
    flagged = flag > 0
    receive_line(R0)
    stage(R1, apply_to(R0)[0])
    send(R1)
    keep(X0, input_blocks(2))
    send_peers(X0)
    payload = jnp.zeros((cases, tb), jnp.float32)
    payload = gram_of(payload, (0, 1, 4, 5))
    receive(P1)
    advance()
    stage(P2, apply_to(P1)[0])
    send(P2)
    payload = gram_of(payload, (0, 1, 2, 4, 5))
    receive(R1)
    for b, value in enumerate(apply_to(R1)[0]):
        own[SENT + 1][b] = value
    payload = gram_of(payload, (0, 1, 2, 4, 5, 6))
    receive_peers(X0)
    send_line(X0)
    while len(passed) < len(reaches):
        advance()
    receive(P2)
    for b, value in enumerate(apply_to(P2)[0]):
        own[SENT][b] = value
    payload = gram_of(payload, range(WIDTH))
    assert len(done) == len(MOMENTS)

    payload = jnp.sum(payload, axis=0, keepdims=True)
    gram_own[0] = payload
    gram_all[me] = payload

    def gram_copy(dd, rr):
        return pltpu.make_async_remote_copy(
            src_ref=gram_own.at[0],
            dst_ref=gram_all.at[me],
            send_sem=gram_send,
            recv_sem=gram_recv,
            device_id=(dd, rr),
            device_id_type=MESH,
        )

    @pl.loop(1, parts)
    def _(k):
        to = far_first(k)
        for rr in others + [r]:
            gram_copy(to, rr).start()

    for rr in others:
        gram_copy(d, rr).start()

    receive_line(X0)
    for b, value in enumerate(apply_to(X0)[0]):
        image[b] = jnp.where(flagged, vec_in[3, :, b, :] - value, 0.0)
    for v in range(SENT):
        sent(v)

    foreign = gram_all.at[pl.ds(0, parts * split - 1)]
    arrived(foreign, gram_send)
    arrived(foreign, gram_recv)

    whole = jnp.broadcast_to(jnp.sum(gram_all[...], axis=0), (cases, tb))
    entries = [
        jnp.broadcast_to(
            jnp.sum(jnp.where(entry_of == cases * e, whole, 0.0), axis=1, keepdims=True),
            (cases, tb),
        )
        for e in range(len(MOMENTS))
    ]
    gram = {pair: entries[ENTRY[moment_of(*pair)]] for pair in PAIRS}
    iterate_c, residual_c, direction_c = coefficients(gram)
    shifted_c = shifted_of(iterate_c)
    replace_c = {
        i: jnp.where(flagged, -shifted_c[i], w) if i in shifted_c else jnp.where(flagged, 0.0, w)
        for i, w in residual_c.items()
    }
    for b in range(own_rows):
        blocks = [ref[b] for ref in basis]

        def combine(total, weights_of):
            for i, w in weights_of.items():
                total = blocks[i] * w if total is None else total + blocks[i] * w
            return total

        out_ref[0, :, b, :] = combine(vec_in[2, :, b, :], iterate_c)
        out_ref[1, :, b, :] = combine(image[b], replace_c)
        out_ref[2, :, b, :] = combine(None, direction_c)


def write_out(made_ref, *refs):
    outs, sem = refs[:-1], refs[-1]
    copies = [
        pltpu.make_async_copy(made_ref.at[i], ref, sem.at[i]) for i, ref in enumerate(outs)
    ]
    for copy in copies:
        copy.start()
    for copy in copies:
        copy.wait()


def body(parts, split, tiles, rows, cols, sends, flags, right, iterate, residual, direction):
    cases, own_rows, tb = residual.shape
    gh = sends.shape[2]
    count = tiles.shape[0]
    f32 = jnp.float32
    dma = pltpu.SemaphoreType.DMA
    hbm = pl.BlockSpec(memory_space=pltpu.HBM)
    vmem = pl.BlockSpec(memory_space=pltpu.VMEM)
    scratch = (
        [pltpu.VMEM((split * own_rows + 2 * gh, cases, tb), f32)] * SENT
        + [pltpu.VMEM((own_rows, cases, tb), f32)] * (SENT + 3)
        + [pltpu.VMEM((2, gh, cases, tb), f32)] * SENT
        + [pltpu.VMEM((2, split, gh, cases, tb), f32)] * WIDE
        + [pltpu.VMEM((2, gh, cases, tb), f32)] * (SENT - WIDE)
        + [
            pltpu.VMEM((count, tb, tb), f32),
            pltpu.VMEM((count // 2, 2 * tb, 2 * tb), jnp.bfloat16),
            pltpu.VMEM((4, cases, own_rows, tb), f32),
            pltpu.VMEM((1, 1, tb), f32),
            pltpu.VMEM((parts * split, 1, tb), f32),
            pltpu.SMEM(rows.shape, jnp.int32),
            pltpu.SMEM(cols.shape, jnp.int32),
            pltpu.SMEM(sends.shape, jnp.int32),
            pltpu.SMEM(flags.shape, jnp.int32),
            dma((4,)),
            dma((4,)),
            dma((4,)),
            dma((SENT,)),
            dma((SENT,)),
            dma((SENT, 2)),
            dma((SENT, 2)),
            dma,
            dma,
            pltpu.SemaphoreType.REGULAR((max(parts.bit_length(), 1),)),
        ]
    )
    made = pl.pallas_call(
        functools.partial(kernel, parts, split),
        out_shape=pltpu.VMEM((3, cases, own_rows, tb), f32),
        in_specs=[hbm] * 9,
        out_specs=vmem,
        scratch_shapes=scratch,
        compiler_params=pltpu.CompilerParams(
            collective_id=0, has_side_effects=True, vmem_limit_bytes=63 * 1024 * 1024
        ),
    )(rows, cols, sends, flags, tiles, direction, residual, iterate, right)
    return pl.pallas_call(
        write_out,
        out_shape=[jax.ShapeDtypeStruct(residual.shape, f32)] * 3,
        in_specs=[vmem],
        out_specs=[hbm] * 3,
        scratch_shapes=[dma((3,))],
    )(pltpu.with_memory_space_constraint(made, pltpu.VMEM))


def solution(mesh):
    both = ("dom", "rhs")
    vec = P(None, both, None)
    placed = (P(both, None, None), P(both), P(both), P("dom", None, None), P(), vec, vec, vec, vec)
    return jax.shard_map(
        functools.partial(body, mesh.shape["dom"], mesh.shape["rhs"]),
        mesh=mesh,
        in_specs=placed,
        out_specs=(vec, vec, vec),
        check_vma=False,
    )
```
